32 devices in a mesh: pass: 2 (over y), az: 8 (over z, x), rg: 2 (over core).
Axes of the slice: x: 2, y: 2, z: 4, core: 2. Of those that a mesh axis runs over, the one named last changes fastest.
Arguments:
- reference_slc: bfloat16 [2, 4096, 10240], P(None, ('pass', 'az'), 'rg'), parts along dimension 1, may hold values from -8 to 8, as said below
- secondary_slc: bfloat16 [2, 4096, 10240], P(None, ('pass', 'az'), 'rg'), parts along dimension 1, may hold values from -20 to 20, as said below
- line_target: int32 [1024], P(('pass', 'az')), parts along dimension 0, may hold values from 0 to 511, as said below
- seam_partner: int32 [1024], P(('pass', 'az')), parts along dimension 0, may hold values from -1 to 63, as said below
- mask_level: int32 [1024, 512], P(('pass', 'az'), 'rg'), parts along dimension 0, may hold values from 0 to 3
Outputs:
- unwrapped: float32 [1024, 512], P(('pass', 'az'), 'rg'), parts along dimension 0
- residual: float32 [1024, 512], P(('pass', 'az'), 'rg'), parts along dimension 0
The draws below stay inside these ranges and needn't reach their ends.
There are 2 independent parts, one for each index of `pass`. The reference program is written for one: setup_inputs(seed, part) draws one part's arguments, and reference() takes and returns one part's arrays. A program takes and returns all parts, laid end to end along the dimension named above; each array names one. Nothing has to cross between parts.
Inputs may be any that keep to these rules, and one draw needn't show every extreme that they name: `reference_slc`: real and imaginary planes of complex samples. `secondary_slc`: real and imaginary planes of complex samples. `line_target`: A permutation of the 512 grid rows, indexed by look row in acquisition order. Every owner of 64 grid rows receives exactly 64 look rows; no owner receives more than 16 look rows from one device, and every device sends exactly 16 look rows to at least one owner. `seam_partner`: -1 where a grid row has no partner, else the index within the next block of 64 grid rows of the row that images the same ground; the partners within a block are distinct, and the last 64 rows have none.
All inputs are finite; a program needn't handle non-finite values.
Results may differ from the reference program's by a relative error of at most 0.0003.
Values sent between devices are 32-bit elements; how exact they have to be, the bound alone decides.
A program may use at most 192 MiB of HBM per device.

```python
import math
import jax
import jax.numpy as jnp
from jax import lax

LOOK_AZ = 4
LOOK_RG = 20
R_DEV = 64
ITERS = 2
ROWS = 512
COLS = 512
N_AZ = 8


def slc_pair(key):
    line_total = LOOK_AZ * ROWS
    sample_total = LOOK_RG * COLS
    base_key = jax.random.fold_in(key, 4101)
    ref_key, phase_key, noise_key = jax.random.split(base_key, 3)
    shape_full = (2, line_total, sample_total)
    ref_planes = jnp.clip(jax.random.normal(ref_key, shape_full, jnp.float32), -6.0, 6.0)
    noise_planes = jnp.clip(jax.random.normal(noise_key, shape_full, jnp.float32), -6.0, 6.0)
    phase_cells = jax.random.uniform(phase_key, (ROWS, COLS), jnp.float32, -math.pi, math.pi)
    phase_full = jnp.repeat(jnp.repeat(phase_cells, LOOK_AZ, axis=0), LOOK_RG, axis=1)
    spread = 0.2 + 1.5 * jnp.arange(line_total, dtype=jnp.float32)[:, None] / line_total
    cosine = jnp.cos(phase_full)
    sine = jnp.sin(phase_full)
    sec_real = cosine * ref_planes[0] - sine * ref_planes[1] + spread * noise_planes[0]
    sec_imag = sine * ref_planes[0] + cosine * ref_planes[1] + spread * noise_planes[1]
    return (ref_planes, jnp.stack([sec_real, sec_imag]))


def draw_reference_slc(key, part):
    return slc_pair(key)[0].astype(jnp.bfloat16)


def draw_secondary_slc(key, part):
    return slc_pair(key)[1].astype(jnp.bfloat16)


def draw_line_target(key, part):
    device_total = N_AZ
    row_total = R_DEV
    capacity = max(2, 2 * row_total // device_total)
    size_key, offset_key, order_key = jax.random.split(jax.random.fold_in(key, 733), 3)
    group_sizes = jax.random.randint(size_key, (device_total,), capacity // 2, capacity + 1)
    group_sizes = group_sizes.at[0].set(capacity)
    group_ends = jnp.minimum(jnp.cumsum(group_sizes), row_total)
    offsets = jax.random.permutation(offset_key, device_total)
    slot_of = jax.vmap(lambda b: jax.random.permutation(jax.random.fold_in(order_key, b), row_total))(jnp.arange(device_total))
    group_of = jnp.sum((group_ends[None, None, :] <= slot_of[:, :, None]).astype(jnp.int32), axis=2)
    owner_dev = (jnp.arange(device_total)[:, None] + offsets[group_of]) % device_total
    return (owner_dev * row_total + slot_of).reshape(-1).astype(jnp.int32)


def draw_seam_partner(key, part):
    device_total = N_AZ
    row_total = R_DEV
    count_key, match_key = jax.random.split(jax.random.fold_in(key, 977))
    seam_count = jax.random.randint(count_key, (device_total,), row_total // 4, row_total // 2 + 1)
    matches = jax.vmap(lambda b: jax.random.permutation(jax.random.fold_in(match_key, b), row_total))(jnp.arange(device_total))
    local_row = jnp.arange(row_total)
    position = local_row[None, :] - (row_total - seam_count[:, None])
    chosen = jnp.take_along_axis(matches, jnp.clip(position, 0, row_total - 1), axis=1)
    linked = (position >= 0) & (jnp.arange(device_total)[:, None] < device_total - 1)
    return jnp.where(linked, chosen, -1).reshape(-1).astype(jnp.int32)


def set_ends(values, rng, low, high):
    longest = values.shape.index(max(values.shape))
    spots = []
    for shift in (0, 1):
        where = [jax.random.randint(jax.random.fold_in(rng, axis), (), 0, length) for axis, length in enumerate(values.shape)]
        where[longest] = (where[longest] + shift) % values.shape[longest]
        spots.append(tuple(where))
    return values.at[spots[0]].set(low).at[spots[1]].set(high)


def setup_inputs(seed: int = 0, part: int = 0) -> dict:
    key_list = jax.random.split(jax.random.key(seed), 6)
    own_keys = jax.random.split(jax.random.fold_in(key_list[5], part), 6)
    reference_slc = draw_reference_slc(jax.random.fold_in(jax.random.fold_in(key_list[5], part), 71), part)
    secondary_slc = draw_secondary_slc(jax.random.fold_in(jax.random.fold_in(key_list[5], part), 71), part)
    line_target = draw_line_target(jax.random.fold_in(jax.random.fold_in(key_list[5], part), 71), part)
    seam_partner = draw_seam_partner(jax.random.fold_in(jax.random.fold_in(key_list[5], part), 71), part)
    mask_level = set_ends(jax.random.randint(own_keys[4], (ROWS, COLS), 0, 4), jax.random.fold_in(own_keys[4], 1), 0, 3).astype(jnp.int32)
    return dict(reference_slc=reference_slc, secondary_slc=secondary_slc, line_target=line_target, seam_partner=seam_partner, mask_level=mask_level)


FULL_PRECISION = lax.Precision.HIGHEST
EPSILON = 1e-06

def dct_table(freq_index, place_index, length):
    product = (2 * place_index[None, :] + 1) * freq_index[:, None] % (4 * length)
    norm_factor = jnp.where(freq_index == 0, math.sqrt(1.0 / length), math.sqrt(2.0 / length)).astype(jnp.float32)
    return norm_factor[:, None] * jnp.cos(product.astype(jnp.float32) * (math.pi / (2.0 * length)))

def eigenvalues(freq_index, length):
    return 4.0 * jnp.sin(freq_index.astype(jnp.float32) * (math.pi / (2.0 * length))) ** 2

def neighbours(padded):
    return (padded[..., :-2, 1:-1], padded[..., 2:, 1:-1], padded[..., 1:-1, :-2], padded[..., 1:-1, 2:])

def matmul(left, right):
    return jnp.dot(left, right, precision=FULL_PRECISION, preferred_element_type=jnp.float32)

def reference(reference_slc, secondary_slc, line_target, seam_partner, mask_level):
    ref_real = reference_slc[0].astype(jnp.float32)
    ref_imag = reference_slc[1].astype(jnp.float32)
    sec_real = secondary_slc[0].astype(jnp.float32)
    sec_imag = secondary_slc[1].astype(jnp.float32)
    planes = jnp.stack([ref_real * sec_real + ref_imag * sec_imag, ref_imag * sec_real - ref_real * sec_imag, ref_real * ref_real + ref_imag * ref_imag, sec_real * sec_real + sec_imag * sec_imag])
    look_stack = planes.reshape(4, ROWS, LOOK_AZ, COLS, LOOK_RG).sum(axis=(2, 4))
    gridded = jnp.zeros((4, ROWS, COLS), jnp.float32).at[:, line_target].set(look_stack)
    row_index = jnp.arange(ROWS, dtype=jnp.int32)
    partner_row = jnp.minimum((row_index // R_DEV + 1) * R_DEV + jnp.maximum(seam_partner, 0), ROWS - 1).astype(jnp.int32)
    combined = gridded + jnp.where((seam_partner >= 0)[None, :, None], gridded[:, partner_row], 0.0)
    magnitude = jnp.sqrt(combined[2] * combined[3]) + EPSILON
    weight = (1 + mask_level).astype(jnp.float32) * 0.25
    fields = jnp.stack([combined[0] / magnitude, combined[1] / magnitude, weight])
    padded = jnp.pad(fields, ((0, 0), (1, 1), (1, 1)))
    beside_all = neighbours(padded)
    edge_weights = [weight * item[2] for item in beside_all]
    right_side = jnp.zeros((ROWS, COLS), jnp.float32)
    for edge, item in zip(edge_weights, beside_all):
        right_side = right_side + edge * (fields[1] * item[0] - fields[0] * item[1])
    damping = 0.25 / (R_DEV * R_DEV)

    def apply_operator(values):
        rim = jnp.pad(values, 1)
        result_sum = damping * values
        for edge, item in zip(edge_weights, neighbours(rim)):
            result_sum = result_sum + edge * (values - item)
        return result_sum
    row_freq = jnp.arange(ROWS, dtype=jnp.int32)
    col_freq = jnp.arange(COLS, dtype=jnp.int32)
    row_basis = dct_table(row_freq, row_freq, ROWS)
    col_basis = dct_table(col_freq, col_freq, COLS)
    divisor = eigenvalues(row_freq, ROWS)[:, None] + eigenvalues(col_freq, COLS)[None, :] + damping

    def precondition(values):
        spectrum = matmul(matmul(row_basis, values), col_basis.T) / divisor
        return matmul(matmul(row_basis.T, spectrum), col_basis)
    solution = jnp.zeros((ROWS, COLS), jnp.float32)
    residual = right_side
    precond = precondition(residual)
    direction = precond
    inner_now = jnp.sum(residual * precond)
    for turn_index in range(ITERS):
        image_now = apply_operator(direction)
        step_size = inner_now / jnp.sum(direction * image_now)
        solution = solution + step_size * direction
        residual = residual - step_size * image_now
        if turn_index + 1 < ITERS:
            precond = precondition(residual)
            inner_next = jnp.sum(residual * precond)
            direction = precond + inner_next / inner_now * direction
            inner_now = inner_next
    return (solution, residual)
```

```python
import functools
import math

import jax
import jax.numpy as jnp
import numpy as np
from jax import lax
from jax.experimental import pallas as pl
from jax.experimental.pallas import tpu as pltpu
from jax.sharding import PartitionSpec as P

LOOK_AZ = 4
LOOK_RG = 20
ITERS = 2


FULL_PRECISION = lax.Precision.HIGHEST
EPSILON = 1e-06


def from_behind(value, axis, steps):
    count = lax.axis_size(axis)
    first, last = (max(0, -steps), min(count, count - steps))
    return lax.ppermute(value, axis, [(source, source + steps) for source in range(first, last)])


def with_halo(shard, sides, width):
    for axis, dim in sides:
        peers, length = (lax.axis_size(axis), shard.shape[dim])
        up = [(i, (i + 1) % peers) for i in range(peers - 1)]
        down = [(j, i) for i, j in up]
        last = lax.slice_in_dim(shard, length - width, length, axis=dim)
        first = lax.slice_in_dim(shard, 0, width, axis=dim)
        before = lax.ppermute(last, axis, up)
        after = lax.ppermute(first, axis, down)
        shard = jnp.concatenate([before, shard, after], axis=dim)
    return shard


def dct_table(freq_index, place_index, length):
    product = (2 * place_index[None, :] + 1) * freq_index[:, None] % (4 * length)
    norm_factor = jnp.where(
        freq_index == 0, math.sqrt(1.0 / length), math.sqrt(2.0 / length)
    ).astype(jnp.float32)
    return norm_factor[:, None] * jnp.cos(product.astype(jnp.float32) * (math.pi / (2.0 * length)))


def eigenvalues(freq_index, length):
    return 4.0 * jnp.sin(freq_index.astype(jnp.float32) * (math.pi / (2.0 * length))) ** 2


def neighbours(padded):
    return (
        padded[..., :-2, 1:-1],
        padded[..., 2:, 1:-1],
        padded[..., 1:-1, :-2],
        padded[..., 1:-1, 2:],
    )


def contract(left, right, left_dim, right_dim):
    return lax.dot_general(
        left,
        right,
        (((left_dim,), (right_dim,)), ((), ())),
        precision=FULL_PRECISION,
        preferred_element_type=jnp.float32,
    )


CHUNK = 256


def look_kernel(lines, half, ref_ref, sec_ref, group_ref, line_ref, out_ref):
    step_rows = lines // LOOK_AZ
    width = half // LOOK_RG
    for side in range(out_ref.shape[2] // width):
        total = jnp.zeros((8 * lines, width), jnp.float32)
        for start in range(0, half, CHUNK):
            span = pl.ds(side * half + start, CHUNK)
            mr = ref_ref[0, :, span].astype(jnp.float32)
            mi = ref_ref[1, :, span].astype(jnp.float32)
            sr = sec_ref[0, :, span].astype(jnp.float32)
            si = sec_ref[1, :, span].astype(jnp.float32)
            planes = jnp.concatenate(
                [mr * sr + mi * si, mi * sr - mr * si, mr * mr + mi * mi, sr * sr + si * si], axis=0
            )
            high = planes.astype(jnp.bfloat16)
            low = (planes - high.astype(jnp.float32)).astype(jnp.bfloat16)
            total = total + jnp.dot(
                jnp.concatenate([high, low], axis=0),
                group_ref[pl.ds(start, CHUNK), :],
                preferred_element_type=jnp.float32,
            )
        joined = total[: 4 * lines] + total[4 * lines :]
        sums = jnp.dot(
            line_ref[...], joined, precision=FULL_PRECISION, preferred_element_type=jnp.float32
        )
        for plane in range(4):
            out_ref[plane, :, side * width : (side + 1) * width] = sums[
                plane * step_rows : (plane + 1) * step_rows
            ]


def form_looks(ref_lines, sec_lines, col_count):
    line_count, sample_count = ref_lines.shape[1:]
    lines = 32
    half = 128 * LOOK_RG
    group = (np.arange(half)[:, None] // LOOK_RG == np.arange(128)[None, :]).astype(jnp.bfloat16)
    line_of = (np.arange(4 * lines)[None, :] // LOOK_AZ == np.arange(lines)[:, None]).astype(
        np.float32
    )
    block = pl.BlockSpec((2, lines, sample_count), lambda i: (0, i, 0))
    return pl.pallas_call(
        functools.partial(look_kernel, lines, half),
        grid=(line_count // lines,),
        in_specs=[
            block,
            block,
            pl.BlockSpec(group.shape, lambda i: (0, 0)),
            pl.BlockSpec(line_of.shape, lambda i: (0, 0)),
        ],
        out_specs=pl.BlockSpec((4, lines // LOOK_AZ, col_count), lambda i: (0, i, 0)),
        out_shape=jax.ShapeDtypeStruct((4, line_count // LOOK_AZ, col_count), jnp.float32),
        name="form_looks",
    )(ref_lines, sec_lines, group, line_of)


def single_product(left, right):
    return lax.psum(jnp.sum(left * right), ("az", "rg"))


def on_device(reference_slc, secondary_slc, line_target, seam_partner, mask_level):
    dev_count = lax.axis_size("az")
    rg_count = lax.axis_size("rg")
    az_place = lax.axis_index("az")
    rg_place = lax.axis_index("rg")
    row_count = line_target.shape[0]
    col_count = mask_level.shape[1]
    capacity = max(2, 2 * row_count // dev_count)
    owners = line_target // row_count
    local_index = jnp.arange(row_count, dtype=jnp.int32)
    earlier = (owners[:, None] == owners[None, :]) & (local_index[None, :] < local_index[:, None])
    slot_rank = jnp.sum(earlier.astype(jnp.int32), axis=1)
    slot_index = owners * capacity + slot_rank
    buffer_length = dev_count * capacity
    source_row = jnp.full((buffer_length,), row_count, jnp.int32).at[slot_index].set(local_index)
    positions = (
        jnp.full((1, buffer_length), row_count, jnp.int32)
        .at[0, slot_index]
        .set(line_target % row_count)
    )
    local_sums = form_looks(reference_slc, secondary_slc, col_count)
    sent_sums = jnp.take(local_sums, source_row, axis=1, mode="fill", fill_value=0.0)
    got_sums, got_positions = (
        lax.all_to_all(sent_sums, "az", split_axis=1, concat_axis=1, tiled=True),
        lax.all_to_all(positions, "az", split_axis=1, concat_axis=1, tiled=True),
    )
    gridded = jnp.zeros_like(local_sums).at[:, got_positions[0]].set(got_sums, mode="drop")
    next_block = from_behind(gridded, "az", -1)
    has_partner = seam_partner >= 0
    picked = jnp.take(next_block, jnp.maximum(seam_partner, 0), axis=1)
    combined = gridded + jnp.where(has_partner[None, :, None], picked, 0.0)
    magnitude = jnp.sqrt(combined[2] * combined[3]) + EPSILON
    weight = (1 + mask_level).astype(jnp.float32) * 0.25
    fields = jnp.stack([combined[0] / magnitude, combined[1] / magnitude, weight])
    padded = with_halo(fields, (("az", 1), ("rg", 2)), 1)
    beside_all = neighbours(padded)
    edge_weights = [weight * item[2] for item in beside_all]
    right_side = jnp.zeros((row_count, col_count), jnp.float32)
    for edge, item in zip(edge_weights, beside_all):
        right_side = right_side + edge * (fields[1] * item[0] - fields[0] * item[1])
    damping = 0.25 / (row_count * row_count)
    grid_rows = row_count * dev_count
    grid_cols = col_count * rg_count
    my_cols = rg_place * col_count + jnp.arange(col_count, dtype=jnp.int32)
    column_width = col_count // dev_count
    all_rows = jnp.arange(grid_rows, dtype=jnp.int32)
    full_basis = dct_table(all_rows, all_rows, grid_rows)
    pencil_cols = (
        rg_place * col_count + az_place * column_width + jnp.arange(column_width, dtype=jnp.int32)
    )
    pencil_divisor = (
        eigenvalues(pencil_cols, grid_cols)[:, None]
        + eigenvalues(all_rows, grid_rows)[None, :]
        + damping
    )

    def precondition(values):
        basis_block = dct_table(
            jnp.arange(col_count * lax.axis_size("rg"), dtype=jnp.int32), my_cols, grid_cols
        )
        range_spectrum = lax.psum_scatter(
            contract(basis_block, values, 1, 1), "rg", scatter_dimension=0, tiled=True
        )
        pencil = lax.all_to_all(range_spectrum, "az", split_axis=0, concat_axis=1, tiled=True)
        filtered = contract(pencil, full_basis, 1, 1) / pencil_divisor
        restored = contract(filtered, full_basis, 1, 0)
        back_columns = lax.all_to_all(restored, "az", split_axis=1, concat_axis=0, tiled=True)
        basis_block = dct_table(
            my_cols, jnp.arange(col_count * lax.axis_size("rg"), dtype=jnp.int32), grid_cols
        )
        return lax.psum_scatter(
            contract(basis_block, back_columns, 0, 0), "rg", scatter_dimension=0, tiled=True
        ).T

    solution = jnp.zeros((row_count, col_count), jnp.float32)
    residual = right_side
    precond = precondition(residual)
    direction = precond
    inner_now = single_product(residual, precond)
    for turn_index in range(ITERS):
        rim = with_halo(direction, (("az", 0), ("rg", 1)), 1)
        result_sum = damping * direction
        for apply_edge, apply_item in zip(edge_weights, neighbours(rim)):
            result_sum = result_sum + apply_edge * (direction - apply_item)
        step_size = inner_now / lax.psum(jnp.sum(direction * result_sum), ("az", "rg"))
        solution = solution + step_size * direction
        residual = residual - step_size * result_sum
        if turn_index + 1 < ITERS:
            precond = precondition(residual)
            inner_next = single_product(residual, precond)
            direction = precond + inner_next / inner_now * direction
            inner_now = inner_next
    return (solution, residual)


def solution(mesh):
    in_specs = (
        P(None, ("pass", "az"), "rg"),
        P(None, ("pass", "az"), "rg"),
        P(("pass", "az")),
        P(("pass", "az")),
        P(("pass", "az"), "rg"),
    )
    out_specs = (P(("pass", "az"), "rg"), P(("pass", "az"), "rg"))
    return jax.shard_map(
        on_device, mesh=mesh, in_specs=in_specs, out_specs=out_specs, check_vma=False
    )
```

```python
import functools
import math

import jax
import jax.numpy as jnp
import numpy as np
from jax import lax
from jax.experimental import pallas as pl
from jax.experimental.pallas import tpu as pltpu
from jax.sharding import PartitionSpec as P

LOOK_AZ = 4
LOOK_RG = 20
ITERS = 2


FULL_PRECISION = lax.Precision.HIGHEST
EPSILON = 1e-06


def from_behind(value, axis, steps):
    count = lax.axis_size(axis)
    first, last = (max(0, -steps), min(count, count - steps))
    return lax.ppermute(value, axis, [(source, source + steps) for source in range(first, last)])


def with_halo(shard, sides, width):
    for axis, dim in sides:
        peers, length = (lax.axis_size(axis), shard.shape[dim])
        up = [(i, (i + 1) % peers) for i in range(peers - 1)]
        down = [(j, i) for i, j in up]
        last = lax.slice_in_dim(shard, length - width, length, axis=dim)
        first = lax.slice_in_dim(shard, 0, width, axis=dim)
        before = lax.ppermute(last, axis, up)
        after = lax.ppermute(first, axis, down)
        shard = jnp.concatenate([before, shard, after], axis=dim)
    return shard


def dct_table(freq_index, place_index, length):
    product = (2 * place_index[None, :] + 1) * freq_index[:, None] % (4 * length)
    norm_factor = jnp.where(
        freq_index == 0, math.sqrt(1.0 / length), math.sqrt(2.0 / length)
    ).astype(jnp.float32)
    return norm_factor[:, None] * jnp.cos(product.astype(jnp.float32) * (math.pi / (2.0 * length)))


def eigenvalues(freq_index, length):
    return 4.0 * jnp.sin(freq_index.astype(jnp.float32) * (math.pi / (2.0 * length))) ** 2


def neighbours(padded):
    return (
        padded[..., :-2, 1:-1],
        padded[..., 2:, 1:-1],
        padded[..., 1:-1, :-2],
        padded[..., 1:-1, 2:],
    )


def contract(left, right, left_dim, right_dim):
    return lax.dot_general(
        left,
        right,
        (((left_dim,), (right_dim,)), ((), ())),
        precision=FULL_PRECISION,
        preferred_element_type=jnp.float32,
    )


CHUNK = 256


def look_kernel(lines, half, ref_ref, sec_ref, group_ref, line_ref, out_ref):
    step_rows = lines // LOOK_AZ
    width = half // LOOK_RG
    for side in range(out_ref.shape[2] // width):
        total = jnp.zeros((8 * lines, width), jnp.float32)
        for start in range(0, half, CHUNK):
            span = pl.ds(side * half + start, CHUNK)
            mr = ref_ref[0, :, span].astype(jnp.float32)
            mi = ref_ref[1, :, span].astype(jnp.float32)
            sr = sec_ref[0, :, span].astype(jnp.float32)
            si = sec_ref[1, :, span].astype(jnp.float32)
            planes = jnp.concatenate(
                [mr * sr + mi * si, mi * sr - mr * si, mr * mr + mi * mi, sr * sr + si * si], axis=0
            )
            high = planes.astype(jnp.bfloat16)
            low = (planes - high.astype(jnp.float32)).astype(jnp.bfloat16)
            total = total + jnp.dot(
                jnp.concatenate([high, low], axis=0),
                group_ref[pl.ds(start, CHUNK), :],
                preferred_element_type=jnp.float32,
            )
        joined = total[: 4 * lines] + total[4 * lines :]
        sums = jnp.dot(
            line_ref[...], joined, precision=FULL_PRECISION, preferred_element_type=jnp.float32
        )
        for plane in range(4):
            out_ref[plane, :, side * width : (side + 1) * width] = sums[
                plane * step_rows : (plane + 1) * step_rows
            ]


def form_looks(ref_lines, sec_lines, col_count):
    line_count, sample_count = ref_lines.shape[1:]
    lines = 32
    half = 128 * LOOK_RG
    group = (np.arange(half)[:, None] // LOOK_RG == np.arange(128)[None, :]).astype(jnp.bfloat16)
    line_of = (np.arange(4 * lines)[None, :] // LOOK_AZ == np.arange(lines)[:, None]).astype(
        np.float32
    )
    block = pl.BlockSpec((2, lines, sample_count), lambda i: (0, i, 0))
    return pl.pallas_call(
        functools.partial(look_kernel, lines, half),
        grid=(line_count // lines,),
        in_specs=[
            block,
            block,
            pl.BlockSpec(group.shape, lambda i: (0, 0)),
            pl.BlockSpec(line_of.shape, lambda i: (0, 0)),
        ],
        out_specs=pl.BlockSpec((4, lines // LOOK_AZ, col_count), lambda i: (0, i, 0)),
        out_shape=jax.ShapeDtypeStruct((4, line_count // LOOK_AZ, col_count), jnp.float32),
        name="form_looks",
    )(ref_lines, sec_lines, group, line_of)


class Exchange:
    def __init__(self, send_sems, recv_sems):
        self.send_sems, self.recv_sems = send_sems, recv_sems
        self.used = 0

    def copy(self, source, target, device):
        index = self.used
        self.used += 1
        return pltpu.make_async_remote_copy(
            src_ref=source,
            dst_ref=target,
            send_sem=self.send_sems.at[index],
            recv_sem=self.recv_sems.at[index],
            device_id=device,
            device_id_type=pl.DeviceIdType.MESH,
        )


def full_dot(left, right, dims=(1, 0)):
    return lax.dot_general(
        left,
        right,
        (((dims[0],), (dims[1],)), ((), ())),
        precision=FULL_PRECISION,
        preferred_element_type=jnp.float32,
    )


def iota(shape, dim):
    return lax.broadcasted_iota(jnp.int32, shape, dim)


def unwrap_kernel(
    peers,
    capacity,
    damping,
    sums_ref,
    target_row_ref,
    target_col_ref,
    seam_ref,
    mask_ref,
    basis_ref,
    lam_row_ref,
    lam_col_ref,
    out_ref,
    res_ref,
    slot_send,
    slot_recv,
    place_send,
    place_recv,
    grid_own,
    grid_next,
    fields,
    spec_send,
    spec_recv,
    back_send,
    back_recv,
    dot_send,
    dot_recv,
    send_sems,
    recv_sems,
):
    me = lax.axis_index("az")
    core = lax.axis_index("rg")
    other = 1 - core
    last = peers - 1
    rows, cols = mask_ref.shape
    length = basis_ref.shape[0]
    slots = peers * capacity
    pencil = cols // peers
    exchange = Exchange(send_sems, recv_sems)
    sent = []

    def at(az, rg):
        return (lax.axis_index("pass"), az, rg)

    def ahead(offset):
        return lax.rem(me + offset, peers)

    def behind(offset):
        return lax.rem(me + peers - offset, peers)

    barrier = pltpu.get_barrier_semaphore()
    for offset in range(peers):
        for side in (core, other):
            if offset or side is other:
                pl.semaphore_signal(
                    barrier,
                    inc=1,
                    device_id=at(ahead(offset), side),
                    device_id_type=pl.DeviceIdType.MESH,
                )

    target_row = target_row_ref[...]
    target_col = target_col_ref[...]
    owner_row = target_row // rows
    owner_col = target_col // rows
    same = owner_col == owner_row
    low_index = iota((rows, rows), 0)
    high_index = iota((rows, rows), 1)
    rank_row = jnp.sum(
        jnp.where(same & (low_index < high_index), 1, 0), axis=0, keepdims=True
    )
    rank_col = jnp.sum(
        jnp.where(same & (high_index < low_index), 1, 0), axis=1, keepdims=True
    )
    choose = jnp.where(
        iota((slots, rows), 0) == owner_row * capacity + rank_row, 1.0, 0.0
    ).astype(jnp.float32)
    place = (target_col - owner_col * rows + 1).astype(jnp.float32)
    lane = iota((rows, slots), 1)
    here = lane == me * capacity + rank_col
    for dest in range(peers):
        line = jnp.sum(
            jnp.where(here & (owner_col == dest), place, 0.0), axis=0, keepdims=True
        )
        place_send[dest] = jnp.broadcast_to(line, (8, slots))
    for plane in range(4):
        chosen = full_dot(choose, sums_ref[plane])
        slot_send[plane] = chosen.reshape(peers, capacity, cols)

    pl.semaphore_wait(barrier, 2 * peers - 1)
    place_copies = []
    for offset in range(1, peers):
        copy = exchange.copy(
            place_send.at[ahead(offset)], place_recv.at[me], at(ahead(offset), core)
        )
        copy.start()
        place_copies.append(copy)
    slot_copies = []
    for plane in range(4):
        row_copies = []
        for offset in range(1, peers):
            copy = exchange.copy(
                slot_send.at[plane, ahead(offset)],
                slot_recv.at[plane, me],
                at(ahead(offset), core),
            )
            copy.start()
            row_copies.append(copy)
        slot_copies.append(row_copies)
        slot_recv[plane, me] = slot_send[plane, me]
        sent += row_copies
    place_recv[me] = place_send[me]
    sent += place_copies

    seam_pick = jnp.where(seam_ref[...] == iota((rows, rows), 1), 1.0, 0.0).astype(jnp.float32)
    for copy in place_copies:
        copy.wait_recv()
    places = place_recv[0]
    for source in range(1, peers):
        places = places + place_recv[source]
    scatter = jnp.where(
        places[0:1] == (iota((rows, slots), 0) + 1).astype(jnp.float32), 1.0, 0.0
    ).astype(jnp.float32)
    seam_copies = []

    @pl.when(me == last)
    def _():
        grid_next[...] = jnp.zeros_like(grid_next)

    for plane in range(4):
        for copy in slot_copies[plane]:
            copy.wait_recv()
        grid_own[plane] = full_dot(scatter, slot_recv[plane].reshape(slots, cols))
        copy = exchange.copy(grid_own.at[plane], grid_next.at[plane], at(behind(1), core))

        @pl.when(me > 0)
        def _():
            copy.start()

        seam_copies.append(copy)

    own_lanes = pl.ds(pl.multiple_of(core * cols, cols), cols)
    fields[2, 8 : 8 + rows, own_lanes] = (1 + mask_ref[...]).astype(jnp.float32) * 0.25
    combined = []
    for plane in range(4):

        @pl.when(me < last)
        def _():
            seam_copies[plane].wait_recv()

        combined.append(grid_own[plane] + full_dot(seam_pick, grid_next[plane]))
    magnitude = jnp.sqrt(combined[2] * combined[3]) + EPSILON
    fields[0, 8 : 8 + rows, own_lanes] = combined[0] / magnitude
    fields[1, 8 : 8 + rows, own_lanes] = combined[1] / magnitude

    @pl.when(me == 0)
    def _():
        fields[:, 0:8, :] = jnp.zeros((3, 8, length), jnp.float32)

    @pl.when(me == last)
    def _():
        fields[:, 8 + rows :, :] = jnp.zeros((3, 8, length), jnp.float32)

    up_copies, down_copies = [], []
    for side in (core, other):
        up_copies.append(
            exchange.copy(
                fields.at[:, pl.ds(8, 8), own_lanes],
                fields.at[:, pl.ds(8 + rows, 8), own_lanes],
                at(behind(1), side),
            )
        )
        down_copies.append(
            exchange.copy(
                fields.at[:, pl.ds(rows, 8), own_lanes],
                fields.at[:, pl.ds(0, 8), own_lanes],
                at(ahead(1), side),
            )
        )

    @pl.when(me > 0)
    def _():
        for copy in up_copies:
            copy.start()

    @pl.when(me < last)
    def _():
        for copy in down_copies:
            copy.start()

    across = exchange.copy(
        fields.at[:, pl.ds(8, rows), own_lanes],
        fields.at[:, pl.ds(8, rows), own_lanes],
        at(me, other),
    )
    across.start()
    across.wait_recv()
    sent.append(across)

    @pl.when(me < last)
    def _():
        for copy in up_copies:
            copy.wait_recv()

    @pl.when(me > 0)
    def _():
        for copy in down_copies:
            copy.wait_recv()

    column = iota((rows, length), 1)

    def beside(values):
        middle = values[8 : 8 + rows]
        return (
            values[7 : 7 + rows],
            values[9 : 9 + rows],
            pltpu.roll(middle, 1, 1),
            pltpu.roll(middle, length - 1, 1),
        )

    weight = fields[2]
    inside = weight[8 : 8 + rows]
    edges = [inside * item for item in beside(weight)]
    edges[2] = jnp.where(column > 0, edges[2], 0.0)
    edges[3] = jnp.where(column < length - 1, edges[3], 0.0)
    real, imag = fields[0], fields[1]
    right_side = jnp.zeros((rows, length), jnp.float32)
    for edge, real_item, imag_item in zip(edges, beside(real), beside(imag)):
        right_side = right_side + edge * (
            imag[8 : 8 + rows] * real_item - real[8 : 8 + rows] * imag_item
        )

    def operator(values):
        middle = values[8 : 8 + rows]
        result = damping * middle
        for edge, item in zip(edges, beside(values)):
            result = result + edge * (middle - item)
        return result

    first_freq = pl.multiple_of(core * cols + me * pencil, pencil)
    divisor = lam_col_ref[pl.ds(first_freq, pencil), :] + lam_row_ref[...] + damping

    def gather_dots(turn, values):
        row = iota((8, 128), 0)
        tile = jnp.zeros((8, 128), jnp.float32)
        for index, value in enumerate(values):
            tile = jnp.where(row == index, jnp.sum(value, keepdims=True), tile)
        dot_send[turn] = tile
        dot_recv[turn, me] = tile
        copies = []
        for offset in range(1, peers):
            copy = exchange.copy(
                dot_send.at[turn], dot_recv.at[turn, me], at(ahead(offset), core)
            )
            copy.start()
            copies.append(copy)
        sent.extend(copies)

        def finish():
            for copy in copies:
                copy.wait_recv()
            total = dot_recv[turn, 0]
            for source in range(1, peers):
                total = total + dot_recv[turn, source]
            return [total[index : index + 1, 0:1] for index in range(len(values))]

        return finish

    def precondition(turn, values, meanwhile):
        half_basis = basis_ref[pl.ds(pl.multiple_of(core * cols, cols), cols), :]
        spectrum = full_dot(half_basis, values, (1, 1))
        half = pencil // 2
        for dest in range(peers):
            base = dest * pencil
            spec_send[turn, dest] = jnp.concatenate(
                [spectrum[base : base + half], spectrum[base + half : base + pencil]], axis=1
            )
        copies = []
        for offset in range(1, peers):
            copy = exchange.copy(
                spec_send.at[turn, ahead(offset)],
                spec_recv.at[turn, me],
                at(ahead(offset), core),
            )
            copy.start()
            copies.append(copy)
        spec_recv[turn, me] = spec_send[turn, me]
        extra = meanwhile()
        for copy in copies:
            copy.wait_recv()
        sent.extend(copies)
        blocks = [spec_recv[turn, source] for source in range(peers)]
        columns = jnp.concatenate(
            [
                jnp.concatenate([block[:, :rows] for block in blocks], axis=1),
                jnp.concatenate([block[:, rows:] for block in blocks], axis=1),
            ],
            axis=0,
        )
        filtered = full_dot(columns, basis_ref[...], (1, 1)) / divisor
        restored = full_dot(filtered, basis_ref[...])
        margin = jnp.zeros((pencil, rows // 2), jnp.float32)
        padded = jnp.concatenate([margin, restored, margin], axis=1)
        for dest in range(peers):
            back_send[turn, dest] = padded[:, dest * rows : (dest + 2) * rows]
        copies = []
        for offset in range(1, peers):
            copy = exchange.copy(
                back_send.at[turn, ahead(offset)],
                back_recv.at[turn, core, me],
                at(ahead(offset), core),
            )
            copy.start()
            copies.append(copy)
        back_recv[turn, core, me] = back_send[turn, me]
        relays = [
            exchange.copy(
                back_send.at[turn, me], back_recv.at[turn, core, me], at(me, other)
            )
        ]
        relays[0].start()
        for offset in range(1, peers):
            copies[offset - 1].wait_recv()
            held = back_recv.at[turn, core, behind(offset)]
            relay = exchange.copy(held, held, at(me, other))
            relay.start()
            relays.append(relay)
        for relay in relays:
            relay.wait_recv()
        sent.extend(copies + relays)
        window = back_recv[turn].reshape(length, 2 * rows).T
        start = rows // 2 - 8
        return full_dot(window[start : start + rows + 16], basis_ref[...]), extra

    z0, _ = precondition(0, right_side, lambda: None)
    z0_mid = z0[8 : 8 + rows]
    w0 = operator(z0)
    y0, finish = precondition(
        1, w0, lambda: gather_dots(0, [right_side * z0_mid, z0_mid * w0])
    )
    rho0, energy0 = finish()
    alpha0 = rho0 / energy0
    r1 = right_side - alpha0 * w0
    z1 = z0 - alpha0 * y0
    z1_mid = z1[8 : 8 + rows]
    q1 = operator(z1)
    rho1, energy1, cross = gather_dots(1, [r1 * z1_mid, z1_mid * q1, z0_mid * q1])()
    beta = rho1 / rho0
    alpha1 = rho1 / (energy1 + 2.0 * beta * cross + beta * beta * energy0)
    answer = alpha0 * z0_mid + alpha1 * (z1_mid + beta * z0_mid)
    left = r1 - alpha1 * (q1 + beta * w0)
    out_ref[...] = jnp.where(core == 0, answer[:, :cols], answer[:, cols:])
    res_ref[...] = jnp.where(core == 0, left[:, :cols], left[:, cols:])

    for copy in sent:
        copy.wait_send()

    @pl.when(me > 0)
    def _():
        for copy in seam_copies + up_copies:
            copy.wait_send()

    @pl.when(me < last)
    def _():
        for copy in down_copies:
            copy.wait_send()


def fits_kernel(peers, cores, rows, cols):
    length = rows * peers
    capacity = max(2, 2 * rows // peers)
    return (
        cores == 2
        and rows == 64
        and length == cols * cores
        and length <= 1024
        and peers * capacity == 128
        and cols % (16 * peers) == 0
    )


def unwrap_in_kernel(sums, line_target, seam_partner, mask_level, peers):
    rows, cols = mask_level.shape
    length = rows * peers
    capacity = max(2, 2 * rows // peers)
    damping = 0.25 / (rows * rows)
    freq = np.arange(length)
    angle = (2 * freq[None, :] + 1) * freq[:, None] % (4 * length)
    basis = np.sqrt(np.where(freq == 0, 1.0, 2.0) / length)[:, None] * np.cos(
        angle * (math.pi / (2.0 * length))
    )
    lam = 4.0 * np.sin(freq * (math.pi / (2.0 * length))) ** 2
    pencil = cols // peers
    copies = 4 * (peers - 1) + (peers - 1) + 4 + 5 + 2 * (3 * (peers - 1) + 1) + 2 * (peers - 1)
    vmem = pl.BlockSpec(memory_space=pltpu.VMEM)
    shape = jax.ShapeDtypeStruct((rows, cols), jnp.float32)

    def scratch(*dims):
        return pltpu.VMEM(dims, jnp.float32)

    return pl.pallas_call(
        functools.partial(unwrap_kernel, peers, capacity, damping),
        out_shape=(shape, shape),
        in_specs=[vmem] * 8,
        out_specs=(vmem, vmem),
        scratch_shapes=[
            scratch(4, peers, capacity, cols),
            scratch(4, peers, capacity, cols),
            scratch(peers, 8, 128),
            scratch(peers, 8, 128),
            scratch(4, rows, cols),
            scratch(4, rows, cols),
            scratch(3, rows + 16, length),
            scratch(2, peers, pencil // 2, 2 * rows),
            scratch(2, peers, pencil // 2, 2 * rows),
            scratch(2, peers, pencil, 2 * rows),
            scratch(2, 2, peers, pencil, 2 * rows),
            scratch(2, 8, 128),
            scratch(2, peers, 8, 128),
            pltpu.SemaphoreType.DMA((copies,)),
            pltpu.SemaphoreType.DMA((copies,)),
        ],
        compiler_params=pltpu.CompilerParams(collective_id=0, has_side_effects=True),
        name="unwrap",
    )(
        sums,
        line_target.reshape(1, rows),
        line_target.reshape(rows, 1),
        seam_partner.reshape(rows, 1),
        mask_level,
        basis.astype(np.float32),
        lam.astype(np.float32)[None, :],
        lam.astype(np.float32)[:, None],
    )


def single_product(left, right):
    return lax.psum(jnp.sum(left * right), ("az", "rg"))


def on_device(reference_slc, secondary_slc, line_target, seam_partner, mask_level):
    dev_count = lax.axis_size("az")
    rg_count = lax.axis_size("rg")
    az_place = lax.axis_index("az")
    rg_place = lax.axis_index("rg")
    row_count = line_target.shape[0]
    col_count = mask_level.shape[1]
    local_sums = form_looks(reference_slc, secondary_slc, col_count)
    if fits_kernel(dev_count, rg_count, row_count, col_count):
        return unwrap_in_kernel(local_sums, line_target, seam_partner, mask_level, dev_count)
    capacity = max(2, 2 * row_count // dev_count)
    owners = line_target // row_count
    local_index = jnp.arange(row_count, dtype=jnp.int32)
    earlier = (owners[:, None] == owners[None, :]) & (local_index[None, :] < local_index[:, None])
    slot_rank = jnp.sum(earlier.astype(jnp.int32), axis=1)
    slot_index = owners * capacity + slot_rank
    buffer_length = dev_count * capacity
    source_row = jnp.full((buffer_length,), row_count, jnp.int32).at[slot_index].set(local_index)
    positions = (
        jnp.full((1, buffer_length), row_count, jnp.int32)
        .at[0, slot_index]
        .set(line_target % row_count)
    )
    sent_sums = jnp.take(local_sums, source_row, axis=1, mode="fill", fill_value=0.0)
    got_sums, got_positions = (
        lax.all_to_all(sent_sums, "az", split_axis=1, concat_axis=1, tiled=True),
        lax.all_to_all(positions, "az", split_axis=1, concat_axis=1, tiled=True),
    )
    gridded = jnp.zeros_like(local_sums).at[:, got_positions[0]].set(got_sums, mode="drop")
    next_block = from_behind(gridded, "az", -1)
    has_partner = seam_partner >= 0
    picked = jnp.take(next_block, jnp.maximum(seam_partner, 0), axis=1)
    combined = gridded + jnp.where(has_partner[None, :, None], picked, 0.0)
    magnitude = jnp.sqrt(combined[2] * combined[3]) + EPSILON
    weight = (1 + mask_level).astype(jnp.float32) * 0.25
    fields = jnp.stack([combined[0] / magnitude, combined[1] / magnitude, weight])
    padded = with_halo(fields, (("az", 1), ("rg", 2)), 1)
    beside_all = neighbours(padded)
    edge_weights = [weight * item[2] for item in beside_all]
    right_side = jnp.zeros((row_count, col_count), jnp.float32)
    for edge, item in zip(edge_weights, beside_all):
        right_side = right_side + edge * (fields[1] * item[0] - fields[0] * item[1])
    damping = 0.25 / (row_count * row_count)
    grid_rows = row_count * dev_count
    grid_cols = col_count * rg_count
    my_cols = rg_place * col_count + jnp.arange(col_count, dtype=jnp.int32)
    column_width = col_count // dev_count
    all_rows = jnp.arange(grid_rows, dtype=jnp.int32)
    full_basis = dct_table(all_rows, all_rows, grid_rows)
    pencil_cols = (
        rg_place * col_count + az_place * column_width + jnp.arange(column_width, dtype=jnp.int32)
    )
    pencil_divisor = (
        eigenvalues(pencil_cols, grid_cols)[:, None]
        + eigenvalues(all_rows, grid_rows)[None, :]
        + damping
    )

    def precondition(values):
        basis_block = dct_table(
            jnp.arange(col_count * lax.axis_size("rg"), dtype=jnp.int32), my_cols, grid_cols
        )
        range_spectrum = lax.psum_scatter(
            contract(basis_block, values, 1, 1), "rg", scatter_dimension=0, tiled=True
        )
        pencil = lax.all_to_all(range_spectrum, "az", split_axis=0, concat_axis=1, tiled=True)
        filtered = contract(pencil, full_basis, 1, 1) / pencil_divisor
        restored = contract(filtered, full_basis, 1, 0)
        back_columns = lax.all_to_all(restored, "az", split_axis=1, concat_axis=0, tiled=True)
        basis_block = dct_table(
            my_cols, jnp.arange(col_count * lax.axis_size("rg"), dtype=jnp.int32), grid_cols
        )
        return lax.psum_scatter(
            contract(basis_block, back_columns, 0, 0), "rg", scatter_dimension=0, tiled=True
        ).T

    solution = jnp.zeros((row_count, col_count), jnp.float32)
    residual = right_side
    precond = precondition(residual)
    direction = precond
    inner_now = single_product(residual, precond)
    for turn_index in range(ITERS):
        rim = with_halo(direction, (("az", 0), ("rg", 1)), 1)
        result_sum = damping * direction
        for apply_edge, apply_item in zip(edge_weights, neighbours(rim)):
            result_sum = result_sum + apply_edge * (direction - apply_item)
        step_size = inner_now / lax.psum(jnp.sum(direction * result_sum), ("az", "rg"))
        solution = solution + step_size * direction
        residual = residual - step_size * result_sum
        if turn_index + 1 < ITERS:
            precond = precondition(residual)
            inner_next = single_product(residual, precond)
            direction = precond + inner_next / inner_now * direction
            inner_now = inner_next
    return (solution, residual)


def solution(mesh):
    in_specs = (
        P(None, ("pass", "az"), "rg"),
        P(None, ("pass", "az"), "rg"),
        P(("pass", "az")),
        P(("pass", "az")),
        P(("pass", "az"), "rg"),
    )
    out_specs = (P(("pass", "az"), "rg"), P(("pass", "az"), "rg"))
    return jax.shard_map(
        on_device, mesh=mesh, in_specs=in_specs, out_specs=out_specs, check_vma=False
    )
```

```python
import functools
import math

import jax
import jax.numpy as jnp
import numpy as np
from jax import lax
from jax.experimental import pallas as pl
from jax.experimental.pallas import tpu as pltpu
from jax.sharding import PartitionSpec as P

LOOK_AZ = 4
LOOK_RG = 20
ITERS = 2


FULL_PRECISION = lax.Precision.HIGHEST
EPSILON = 1e-06


def from_behind(value, axis, steps):
    count = lax.axis_size(axis)
    first, last = (max(0, -steps), min(count, count - steps))
    return lax.ppermute(value, axis, [(source, source + steps) for source in range(first, last)])


def with_halo(shard, sides, width):
    for axis, dim in sides:
        peers, length = (lax.axis_size(axis), shard.shape[dim])
        up = [(i, (i + 1) % peers) for i in range(peers - 1)]
        down = [(j, i) for i, j in up]
        last = lax.slice_in_dim(shard, length - width, length, axis=dim)
        first = lax.slice_in_dim(shard, 0, width, axis=dim)
        before = lax.ppermute(last, axis, up)
        after = lax.ppermute(first, axis, down)
        shard = jnp.concatenate([before, shard, after], axis=dim)
    return shard


def dct_table(freq_index, place_index, length):
    product = (2 * place_index[None, :] + 1) * freq_index[:, None] % (4 * length)
    norm_factor = jnp.where(
        freq_index == 0, math.sqrt(1.0 / length), math.sqrt(2.0 / length)
    ).astype(jnp.float32)
    return norm_factor[:, None] * jnp.cos(product.astype(jnp.float32) * (math.pi / (2.0 * length)))


def eigenvalues(freq_index, length):
    return 4.0 * jnp.sin(freq_index.astype(jnp.float32) * (math.pi / (2.0 * length))) ** 2


def neighbours(padded):
    return (
        padded[..., :-2, 1:-1],
        padded[..., 2:, 1:-1],
        padded[..., 1:-1, :-2],
        padded[..., 1:-1, 2:],
    )


def contract(left, right, left_dim, right_dim):
    return lax.dot_general(
        left,
        right,
        (((left_dim,), (right_dim,)), ((), ())),
        precision=FULL_PRECISION,
        preferred_element_type=jnp.float32,
    )


CHUNK = 256


def look_kernel(lines, half, ref_ref, sec_ref, group_ref, line_ref, out_ref):
    step_rows = lines // LOOK_AZ
    width = half // LOOK_RG
    for side in range(out_ref.shape[2] // width):
        total = jnp.zeros((8 * lines, width), jnp.float32)
        for start in range(0, half, CHUNK):
            span = pl.ds(side * half + start, CHUNK)
            mr = ref_ref[0, :, span].astype(jnp.float32)
            mi = ref_ref[1, :, span].astype(jnp.float32)
            sr = sec_ref[0, :, span].astype(jnp.float32)
            si = sec_ref[1, :, span].astype(jnp.float32)
            planes = jnp.concatenate(
                [mr * sr + mi * si, mi * sr - mr * si, mr * mr + mi * mi, sr * sr + si * si], axis=0
            )
            high = planes.astype(jnp.bfloat16)
            low = (planes - high.astype(jnp.float32)).astype(jnp.bfloat16)
            total = total + jnp.dot(
                jnp.concatenate([high, low], axis=0),
                group_ref[pl.ds(start, CHUNK), :],
                preferred_element_type=jnp.float32,
            )
        joined = total[: 4 * lines] + total[4 * lines :]
        sums = jnp.dot(
            line_ref[...], joined, precision=FULL_PRECISION, preferred_element_type=jnp.float32
        )
        for plane in range(4):
            out_ref[plane, :, side * width : (side + 1) * width] = sums[
                plane * step_rows : (plane + 1) * step_rows
            ]


def form_looks(ref_lines, sec_lines, col_count):
    line_count, sample_count = ref_lines.shape[1:]
    lines = 32
    half = 128 * LOOK_RG
    group = (np.arange(half)[:, None] // LOOK_RG == np.arange(128)[None, :]).astype(jnp.bfloat16)
    line_of = (np.arange(4 * lines)[None, :] // LOOK_AZ == np.arange(lines)[:, None]).astype(
        np.float32
    )
    block = pl.BlockSpec((2, lines, sample_count), lambda i: (0, i, 0))
    return pl.pallas_call(
        functools.partial(look_kernel, lines, half),
        grid=(line_count // lines,),
        in_specs=[
            block,
            block,
            pl.BlockSpec(group.shape, lambda i: (0, 0)),
            pl.BlockSpec(line_of.shape, lambda i: (0, 0)),
        ],
        out_specs=pl.BlockSpec((4, lines // LOOK_AZ, col_count), lambda i: (0, i, 0)),
        out_shape=jax.ShapeDtypeStruct((4, line_count // LOOK_AZ, col_count), jnp.float32),
        name="form_looks",
    )(ref_lines, sec_lines, group, line_of)


class Exchange:
    def __init__(self, send_sems, recv_sems):
        self.send_sems, self.recv_sems = send_sems, recv_sems
        self.used = 0

    def copy(self, source, target, device):
        index = self.used
        self.used += 1
        return pltpu.make_async_remote_copy(
            src_ref=source,
            dst_ref=target,
            send_sem=self.send_sems.at[index],
            recv_sem=self.recv_sems.at[index],
            device_id=device,
            device_id_type=pl.DeviceIdType.MESH,
        )


def split(values):
    high = values.astype(jnp.bfloat16)
    rest = values - high.astype(jnp.float32)
    middle = rest.astype(jnp.bfloat16)
    return high, middle, (rest - middle.astype(jnp.float32)).astype(jnp.bfloat16)


def narrow_dot(left, right, dim):
    return lax.dot_general(
        left, right, (((1,), (dim,)), ((), ())), preferred_element_type=jnp.float32
    )


def pick_dot(choose, values):
    high, middle, low = [narrow_dot(choose, part, 0) for part in split(values)]
    return high + (middle + low)


def basis_dot(values, basis, dim):
    count = values.shape[0]
    high, middle, low = split(values)
    first = narrow_dot(jnp.concatenate([high, middle, low], axis=0), basis[0], dim)
    second = narrow_dot(jnp.concatenate([high, middle], axis=0), basis[1], dim)
    third = narrow_dot(high, basis[2], dim)
    small = first[2 * count :] + second[count:] + third
    return first[:count] + ((first[count : 2 * count] + second[:count]) + small)


LINES = 64


def form_block(index, width, ref_held, sec_held, group_ref, hold, looks):
    step_rows = LINES // LOOK_AZ
    lines = pl.ds(index * LINES, LINES)
    total = jnp.zeros((8 * step_rows, width), jnp.float32)
    for start in range(0, ref_held.shape[2], CHUNK):
        parts = []
        for begin in range(start, start + CHUNK, 128):
            span = pl.ds(begin, 128)
            slot = begin // 128
            mr = ref_held[0, lines, span].astype(jnp.float32)
            mi = ref_held[1, lines, span].astype(jnp.float32)
            sr = sec_held[0, lines, span].astype(jnp.float32)
            si = sec_held[1, lines, span].astype(jnp.float32)
            hold[slot, 0:LINES] = mr * sr + mi * si
            hold[slot, LINES : 2 * LINES] = mi * sr - mr * si
            hold[slot, 2 * LINES : 3 * LINES] = mr * mr + mi * mi
            hold[slot, 3 * LINES :] = sr * sr + si * si
            part = hold[slot, pl.ds(0, 4 * step_rows, stride=LOOK_AZ), :]
            for line in range(1, LOOK_AZ):
                part = part + hold[slot, pl.ds(line, 4 * step_rows, stride=LOOK_AZ), :]
            parts.append(part)
        sums = jnp.concatenate(parts, axis=1)
        high = sums.astype(jnp.bfloat16)
        low = (sums - high.astype(jnp.float32)).astype(jnp.bfloat16)
        total = total + jnp.dot(
            jnp.concatenate([high, low], axis=0),
            group_ref[pl.ds(start, CHUNK), :],
            preferred_element_type=jnp.float32,
        )
    joined = total[: 4 * step_rows] + total[4 * step_rows :]
    for plane in range(4):
        looks[plane, pl.ds(index * step_rows, step_rows), :] = joined[
            plane * step_rows : (plane + 1) * step_rows
        ]


def iota(shape, dim):
    return lax.broadcasted_iota(jnp.int32, shape, dim)


def unwrap_kernel(
    peers,
    capacity,
    damping,
    ref_ref,
    sec_ref,
    group_ref,
    target_ref,
    seam_row_ref,
    mask_ref,
    basis_ref,
    lam_row_ref,
    lam_col_ref,
    out_ref,
    ref_held,
    sec_held,
    hold,
    looks,
    load_sems,
    slot_send,
    slot_recv,
    place_send,
    place_recv,
    grid_own,
    grid_next,
    fields,
    spec_send,
    spec_recv,
    back_send,
    back_recv,
    dot_send,
    dot_recv,
    send_sems,
    recv_sems,
):
    me = lax.axis_index("az")
    core = lax.axis_index("rg")
    other = 1 - core
    last = peers - 1
    rows, cols = mask_ref.shape
    length = basis_ref.shape[1]
    slots = peers * capacity
    pencil = cols // peers
    exchange = Exchange(send_sems, recv_sems)
    sent = []

    def at(az, rg):
        return (lax.axis_index("pass"), az, rg)

    def ahead(offset):
        return lax.rem(me + offset, peers)

    def behind(offset):
        return lax.rem(me + peers - offset, peers)

    half = ref_held.shape[3]
    width = half // LOOK_RG
    blocks = rows * LOOK_AZ // LINES
    loads = {}
    for side in range(2):
        for index in range(blocks):
            for which, (source, target) in enumerate(((ref_ref, ref_held), (sec_ref, sec_held))):
                loads[side, index, which] = pltpu.make_async_copy(
                    source.at[:, pl.ds(index * LINES, LINES), pl.ds(side * half, half)],
                    target.at[side, :, pl.ds(index * LINES, LINES), :],
                    load_sems.at[side, index, which],
                )
                loads[side, index, which].start()

    barrier = pltpu.get_barrier_semaphore()
    for offset in range(peers):
        for side in (core, other):
            if offset or side is other:
                pl.semaphore_signal(
                    barrier,
                    inc=1,
                    device_id=at(ahead(offset), side),
                    device_id_type=pl.DeviceIdType.MESH,
                )

    def upright(line):
        diagonal = iota((rows, rows), 0) == iota((rows, rows), 1)
        return jnp.sum(jnp.where(diagonal, line, 0), axis=1, keepdims=True)

    target_row = target_ref[...]
    target_col = upright(target_row)
    owner_row = target_row // rows
    owner_col = target_col // rows
    same = owner_col == owner_row
    low_index = iota((rows, rows), 0)
    high_index = iota((rows, rows), 1)
    rank_row = jnp.sum(
        jnp.where(same & (low_index < high_index), 1, 0), axis=0, keepdims=True
    )
    rank_col = jnp.sum(
        jnp.where(same & (high_index < low_index), 1, 0), axis=1, keepdims=True
    )
    choose = jnp.where(
        iota((slots, rows), 0) == owner_row * capacity + rank_row, 1.0, 0.0
    ).astype(jnp.bfloat16)
    place = (target_col - owner_col * rows + 1).astype(jnp.float32)
    lane = iota((rows, slots), 1)
    here = lane == me * capacity + rank_col
    for dest in range(peers):
        line = jnp.sum(
            jnp.where(here & (owner_col == dest), place, 0.0), axis=0, keepdims=True
        )
        place_send[dest] = jnp.broadcast_to(line, (8, slots))
    pl.semaphore_wait(barrier, 2 * peers - 1)
    place_copies = []
    for offset in range(1, peers):
        copy = exchange.copy(
            place_send.at[ahead(offset)], place_recv.at[me], at(ahead(offset), core)
        )
        copy.start()
        place_copies.append(copy)
    place_recv[me] = place_send[me]
    sent += place_copies
    slot_copies = []
    for side in range(2):
        for index in range(blocks):
            loads[side, index, 0].wait()
            loads[side, index, 1].wait()
            form_block(index, width, ref_held.at[side], sec_held.at[side], group_ref, hold, looks.at[side])
        joined = jnp.concatenate([looks[side, plane] for plane in range(4)], axis=1)
        chosen = pick_dot(choose, joined)
        for plane in range(4):
            slot_send[side, :, plane] = chosen[:, plane * width : (plane + 1) * width].reshape(
                peers, capacity, width
            )
        side_copies = []
        for offset in range(1, peers):
            copy = exchange.copy(
                slot_send.at[side, ahead(offset)],
                slot_recv.at[side, me],
                at(ahead(offset), core),
            )
            copy.start()
            side_copies.append(copy)
        slot_recv[side, me] = slot_send[side, me]
        slot_copies.append(side_copies)
        sent += side_copies

    seam_pick = jnp.where(
        upright(seam_row_ref[...]) == iota((rows, rows), 1), 1.0, 0.0
    ).astype(jnp.bfloat16)
    for copy in place_copies:
        copy.wait_recv()
    places = place_recv[0]
    for source in range(1, peers):
        places = places + place_recv[source]
    scatter = jnp.where(
        places[0:1] == (iota((rows, slots), 0) + 1).astype(jnp.float32), 1.0, 0.0
    ).astype(jnp.bfloat16)
    seam_copies = []

    @pl.when(me == last)
    def _():
        grid_next[...] = jnp.zeros_like(grid_next)

    for side in range(2):
        for copy in slot_copies[side]:
            copy.wait_recv()
        gridded = pick_dot(
            scatter,
            jnp.concatenate(
                [slot_recv[side, :, plane].reshape(slots, width) for plane in range(4)], axis=1
            ),
        )
        grid_own[side] = gridded
        copy = exchange.copy(grid_own.at[side], grid_next.at[side], at(behind(1), core))

        @pl.when(me > 0)
        def _():
            copy.start()

        seam_copies.append(copy)

    own_lanes = pl.ds(pl.multiple_of(core * cols, cols), cols)
    fields[2, 8 : 8 + rows, own_lanes] = (1 + mask_ref[...]).astype(jnp.float32) * 0.25
    combined = []
    for side in range(2):

        @pl.when(me < last)
        def _():
            seam_copies[side].wait_recv()

        combined.append(grid_own[side] + pick_dot(seam_pick, grid_next[side]))
    combined = [
        jnp.concatenate([part[:, plane * width : (plane + 1) * width] for part in combined], axis=1)
        for plane in range(4)
    ]
    magnitude = jnp.sqrt(combined[2] * combined[3]) + EPSILON
    fields[0, 8 : 8 + rows, own_lanes] = combined[0] / magnitude
    fields[1, 8 : 8 + rows, own_lanes] = combined[1] / magnitude

    @pl.when(me == 0)
    def _():
        fields[:, 0:8, :] = jnp.zeros((3, 8, length), jnp.float32)

    @pl.when(me == last)
    def _():
        fields[:, 8 + rows :, :] = jnp.zeros((3, 8, length), jnp.float32)

    up_copies, down_copies = [], []
    for side in (core, other):
        up_copies.append(
            exchange.copy(
                fields.at[:, pl.ds(8, 8), own_lanes],
                fields.at[:, pl.ds(8 + rows, 8), own_lanes],
                at(behind(1), side),
            )
        )
        down_copies.append(
            exchange.copy(
                fields.at[:, pl.ds(rows, 8), own_lanes],
                fields.at[:, pl.ds(0, 8), own_lanes],
                at(ahead(1), side),
            )
        )

    @pl.when(me > 0)
    def _():
        for copy in up_copies:
            copy.start()

    @pl.when(me < last)
    def _():
        for copy in down_copies:
            copy.start()

    across = exchange.copy(
        fields.at[:, pl.ds(8, rows), own_lanes],
        fields.at[:, pl.ds(8, rows), own_lanes],
        at(me, other),
    )
    across.start()
    across.wait_recv()
    sent.append(across)

    @pl.when(me < last)
    def _():
        for copy in up_copies:
            copy.wait_recv()

    @pl.when(me > 0)
    def _():
        for copy in down_copies:
            copy.wait_recv()

    column = iota((rows, length), 1)

    def beside(values):
        middle = values[8 : 8 + rows]
        return (
            values[7 : 7 + rows],
            values[9 : 9 + rows],
            pltpu.roll(middle, 1, 1),
            pltpu.roll(middle, length - 1, 1),
        )

    weight = fields[2]
    inside = weight[8 : 8 + rows]
    edges = [inside * item for item in beside(weight)]
    edges[2] = jnp.where(column > 0, edges[2], 0.0)
    edges[3] = jnp.where(column < length - 1, edges[3], 0.0)
    real, imag = fields[0], fields[1]
    right_side = jnp.zeros((rows, length), jnp.float32)
    for edge, real_item, imag_item in zip(edges, beside(real), beside(imag)):
        right_side = right_side + edge * (
            imag[8 : 8 + rows] * real_item - real[8 : 8 + rows] * imag_item
        )

    def operator(values):
        middle = values[8 : 8 + rows]
        result = damping * middle
        for edge, item in zip(edges, beside(values)):
            result = result + edge * (middle - item)
        return result

    first_freq = pl.multiple_of(core * cols + me * pencil, pencil)
    divisor = lam_col_ref[pl.ds(first_freq, pencil), :] + lam_row_ref[...] + damping

    def gather_dots(turn, values):
        row = iota((8, 128), 0)
        tile = jnp.zeros((8, 128), jnp.float32)
        for index, value in enumerate(values):
            tile = jnp.where(row == index, jnp.sum(value, keepdims=True), tile)
        dot_send[turn] = tile
        dot_recv[turn, me] = tile
        copies = []
        for offset in range(1, peers):
            copy = exchange.copy(
                dot_send.at[turn], dot_recv.at[turn, me], at(ahead(offset), core)
            )
            copy.start()
            copies.append(copy)
        sent.extend(copies)

        def finish():
            for copy in copies:
                copy.wait_recv()
            total = dot_recv[turn, 0]
            for source in range(1, peers):
                total = total + dot_recv[turn, source]
            return [total[index : index + 1, 0:1] for index in range(len(values))]

        return finish

    basis = [basis_ref[part] for part in range(3)]

    def precondition(turn, values, meanwhile):
        half_basis = [basis_ref[part, own_lanes, :] for part in range(3)]
        spectrum = basis_dot(values, half_basis, 1).T
        half = pencil // 2
        for dest in range(peers):
            base = dest * pencil
            spec_send[turn, dest] = jnp.concatenate(
                [spectrum[base : base + half], spectrum[base + half : base + pencil]], axis=1
            )
        copies = []
        for offset in range(1, peers):
            copy = exchange.copy(
                spec_send.at[turn, ahead(offset)],
                spec_recv.at[turn, me],
                at(ahead(offset), core),
            )
            copy.start()
            copies.append(copy)
        spec_recv[turn, me] = spec_send[turn, me]
        extra = meanwhile()
        for copy in copies:
            copy.wait_recv()
        sent.extend(copies)
        blocks = [spec_recv[turn, source] for source in range(peers)]
        columns = jnp.concatenate(
            [
                jnp.concatenate([block[:, :rows] for block in blocks], axis=1),
                jnp.concatenate([block[:, rows:] for block in blocks], axis=1),
            ],
            axis=0,
        )
        filtered = basis_dot(columns, basis, 1) / divisor
        restored = basis_dot(filtered, basis, 0)
        margin = jnp.zeros((pencil, rows // 2), jnp.float32)
        padded = jnp.concatenate([margin, restored, margin], axis=1)
        for dest in range(peers):
            back_send[turn, dest] = padded[:, dest * rows : (dest + 2) * rows]
        copies = []
        for offset in range(1, peers):
            copy = exchange.copy(
                back_send.at[turn, ahead(offset)],
                back_recv.at[turn, core, me],
                at(ahead(offset), core),
            )
            copy.start()
            copies.append(copy)
        back_recv[turn, core, me] = back_send[turn, me]
        relays = [
            exchange.copy(
                back_send.at[turn, me], back_recv.at[turn, core, me], at(me, other)
            )
        ]
        relays[0].start()
        for offset in range(1, peers):
            copies[offset - 1].wait_recv()
            held = back_recv.at[turn, core, behind(offset)]
            relay = exchange.copy(held, held, at(me, other))
            relay.start()
            relays.append(relay)
        for relay in relays:
            relay.wait_recv()
        sent.extend(copies + relays)
        window = back_recv[turn].reshape(length, 2 * rows).T
        start = rows // 2 - 8
        return basis_dot(window[start : start + rows + 16], basis, 0), extra

    z0, _ = precondition(0, right_side, lambda: None)
    z0_mid = z0[8 : 8 + rows]
    w0 = operator(z0)
    y0, finish = precondition(
        1, w0, lambda: gather_dots(0, [right_side * z0_mid, z0_mid * w0])
    )
    rho0, energy0 = finish()
    alpha0 = rho0 / energy0
    r1 = right_side - alpha0 * w0
    z1 = z0 - alpha0 * y0
    z1_mid = z1[8 : 8 + rows]
    q1 = operator(z1)
    rho1, energy1, cross = gather_dots(1, [r1 * z1_mid, z1_mid * q1, z0_mid * q1])()
    beta = rho1 / rho0
    alpha1 = rho1 / (energy1 + 2.0 * beta * cross + beta * beta * energy0)
    answer = alpha0 * z0_mid + alpha1 * (z1_mid + beta * z0_mid)
    left = r1 - alpha1 * (q1 + beta * w0)
    out_ref[0] = jnp.where(core == 0, answer[:, :cols], answer[:, cols:])
    out_ref[1] = jnp.where(core == 0, left[:, :cols], left[:, cols:])

    for copy in sent:
        copy.wait_send()

    @pl.when(me > 0)
    def _():
        for copy in seam_copies + up_copies:
            copy.wait_send()

    @pl.when(me < last)
    def _():
        for copy in down_copies:
            copy.wait_send()


def fits_kernel(peers, cores, rows, cols):
    length = rows * peers
    capacity = max(2, 2 * rows // peers)
    return (
        cores == 2
        and rows == 64
        and length == cols * cores
        and length <= 1024
        and peers * capacity == 128
        and cols % (16 * peers) == 0
        and cols == 256
    )


def unwrap_in_kernel(reference_slc, secondary_slc, line_target, seam_partner, mask_level, peers):
    rows, cols = mask_level.shape
    length = rows * peers
    capacity = max(2, 2 * rows // peers)
    damping = 0.25 / (rows * rows)
    freq = np.arange(length)
    angle = (2 * freq[None, :] + 1) * freq[:, None] % (4 * length)
    basis = np.sqrt(np.where(freq == 0, 1.0, 2.0) / length)[:, None] * np.cos(
        angle * (math.pi / (2.0 * length))
    )
    lam = 4.0 * np.sin(freq * (math.pi / (2.0 * length))) ** 2
    pencil = cols // peers
    half = reference_slc.shape[2] // 2
    width = half // LOOK_RG
    group = (np.arange(half)[:, None] // LOOK_RG == np.arange(width)[None, :]).astype(jnp.bfloat16)
    parts, rest = [], basis
    for _ in range(3):
        parts.append(rest.astype(jnp.bfloat16))
        rest = rest - parts[-1].astype(np.float64)
    hbm = pl.BlockSpec(memory_space=pl.ANY)
    copies = 2 * (peers - 1) + (peers - 1) + 2 + 5 + 2 * (3 * (peers - 1) + 1) + 2 * (peers - 1)
    vmem = pl.BlockSpec(memory_space=pltpu.VMEM)

    def scratch(*dims):
        return pltpu.VMEM(dims, jnp.float32)

    both = pl.pallas_call(
        functools.partial(unwrap_kernel, peers, capacity, damping),
        out_shape=jax.ShapeDtypeStruct((2, rows, cols), jnp.float32),
        in_specs=[hbm] * 2 + [vmem] * 7,
        out_specs=vmem,
        scratch_shapes=[
            pltpu.VMEM((2, 2, rows * LOOK_AZ, half), jnp.bfloat16),
            pltpu.VMEM((2, 2, rows * LOOK_AZ, half), jnp.bfloat16),
            scratch(half // 128, 4 * LINES, 128),
            scratch(2, 4, rows, width),
            pltpu.SemaphoreType.DMA((2, rows * LOOK_AZ // LINES, 2)),
            scratch(2, peers, 4, capacity, width),
            scratch(2, peers, 4, capacity, width),
            scratch(peers, 8, 128),
            scratch(peers, 8, 128),
            scratch(2, rows, 4 * width),
            scratch(2, rows, 4 * width),
            scratch(3, rows + 16, length),
            scratch(2, peers, pencil // 2, 2 * rows),
            scratch(2, peers, pencil // 2, 2 * rows),
            scratch(2, peers, pencil, 2 * rows),
            scratch(2, 2, peers, pencil, 2 * rows),
            scratch(2, 8, 128),
            scratch(2, peers, 8, 128),
            pltpu.SemaphoreType.DMA((copies,)),
            pltpu.SemaphoreType.DMA((copies,)),
        ],
        compiler_params=pltpu.CompilerParams(collective_id=0, has_side_effects=True),
        name="unwrap",
    )(
        reference_slc,
        secondary_slc,
        group,
        line_target.reshape(1, rows),
        seam_partner.reshape(1, rows),
        mask_level,
        np.stack(parts),
        lam.astype(np.float32)[None, :],
        lam.astype(np.float32)[:, None],
    )
    shape = jax.ShapeDtypeStruct((rows, cols), jnp.float32)
    return pl.pallas_call(
        part_kernel,
        out_shape=(shape, shape),
        in_specs=[vmem],
        out_specs=(vmem, vmem),
        name="part",
    )(both)


def part_kernel(both_ref, first_ref, second_ref):
    first_ref[...] = both_ref[0]
    second_ref[...] = both_ref[1]


def single_product(left, right):
    return lax.psum(jnp.sum(left * right), ("az", "rg"))


def on_device(reference_slc, secondary_slc, line_target, seam_partner, mask_level):
    dev_count = lax.axis_size("az")
    rg_count = lax.axis_size("rg")
    az_place = lax.axis_index("az")
    rg_place = lax.axis_index("rg")
    row_count = line_target.shape[0]
    col_count = mask_level.shape[1]
    if fits_kernel(dev_count, rg_count, row_count, col_count):
        return unwrap_in_kernel(
            reference_slc, secondary_slc, line_target, seam_partner, mask_level, dev_count
        )
    local_sums = form_looks(reference_slc, secondary_slc, col_count)
    capacity = max(2, 2 * row_count // dev_count)
    owners = line_target // row_count
    local_index = jnp.arange(row_count, dtype=jnp.int32)
    earlier = (owners[:, None] == owners[None, :]) & (local_index[None, :] < local_index[:, None])
    slot_rank = jnp.sum(earlier.astype(jnp.int32), axis=1)
    slot_index = owners * capacity + slot_rank
    buffer_length = dev_count * capacity
    source_row = jnp.full((buffer_length,), row_count, jnp.int32).at[slot_index].set(local_index)
    positions = (
        jnp.full((1, buffer_length), row_count, jnp.int32)
        .at[0, slot_index]
        .set(line_target % row_count)
    )
    sent_sums = jnp.take(local_sums, source_row, axis=1, mode="fill", fill_value=0.0)
    got_sums, got_positions = (
        lax.all_to_all(sent_sums, "az", split_axis=1, concat_axis=1, tiled=True),
        lax.all_to_all(positions, "az", split_axis=1, concat_axis=1, tiled=True),
    )
    gridded = jnp.zeros_like(local_sums).at[:, got_positions[0]].set(got_sums, mode="drop")
    next_block = from_behind(gridded, "az", -1)
    has_partner = seam_partner >= 0
    picked = jnp.take(next_block, jnp.maximum(seam_partner, 0), axis=1)
    combined = gridded + jnp.where(has_partner[None, :, None], picked, 0.0)
    magnitude = jnp.sqrt(combined[2] * combined[3]) + EPSILON
    weight = (1 + mask_level).astype(jnp.float32) * 0.25
    fields = jnp.stack([combined[0] / magnitude, combined[1] / magnitude, weight])
    padded = with_halo(fields, (("az", 1), ("rg", 2)), 1)
    beside_all = neighbours(padded)
    edge_weights = [weight * item[2] for item in beside_all]
    right_side = jnp.zeros((row_count, col_count), jnp.float32)
    for edge, item in zip(edge_weights, beside_all):
        right_side = right_side + edge * (fields[1] * item[0] - fields[0] * item[1])
    damping = 0.25 / (row_count * row_count)
    grid_rows = row_count * dev_count
    grid_cols = col_count * rg_count
    my_cols = rg_place * col_count + jnp.arange(col_count, dtype=jnp.int32)
    column_width = col_count // dev_count
    all_rows = jnp.arange(grid_rows, dtype=jnp.int32)
    full_basis = dct_table(all_rows, all_rows, grid_rows)
    pencil_cols = (
        rg_place * col_count + az_place * column_width + jnp.arange(column_width, dtype=jnp.int32)
    )
    pencil_divisor = (
        eigenvalues(pencil_cols, grid_cols)[:, None]
        + eigenvalues(all_rows, grid_rows)[None, :]
        + damping
    )

    def precondition(values):
        basis_block = dct_table(
            jnp.arange(col_count * lax.axis_size("rg"), dtype=jnp.int32), my_cols, grid_cols
        )
        range_spectrum = lax.psum_scatter(
            contract(basis_block, values, 1, 1), "rg", scatter_dimension=0, tiled=True
        )
        pencil = lax.all_to_all(range_spectrum, "az", split_axis=0, concat_axis=1, tiled=True)
        filtered = contract(pencil, full_basis, 1, 1) / pencil_divisor
        restored = contract(filtered, full_basis, 1, 0)
        back_columns = lax.all_to_all(restored, "az", split_axis=1, concat_axis=0, tiled=True)
        basis_block = dct_table(
            my_cols, jnp.arange(col_count * lax.axis_size("rg"), dtype=jnp.int32), grid_cols
        )
        return lax.psum_scatter(
            contract(basis_block, back_columns, 0, 0), "rg", scatter_dimension=0, tiled=True
        ).T

    solution = jnp.zeros((row_count, col_count), jnp.float32)
    residual = right_side
    precond = precondition(residual)
    direction = precond
    inner_now = single_product(residual, precond)
    for turn_index in range(ITERS):
        rim = with_halo(direction, (("az", 0), ("rg", 1)), 1)
        result_sum = damping * direction
        for apply_edge, apply_item in zip(edge_weights, neighbours(rim)):
            result_sum = result_sum + apply_edge * (direction - apply_item)
        step_size = inner_now / lax.psum(jnp.sum(direction * result_sum), ("az", "rg"))
        solution = solution + step_size * direction
        residual = residual - step_size * result_sum
        if turn_index + 1 < ITERS:
            precond = precondition(residual)
            inner_next = single_product(residual, precond)
            direction = precond + inner_next / inner_now * direction
            inner_now = inner_next
    return (solution, residual)


def solution(mesh):
    in_specs = (
        P(None, ("pass", "az"), "rg"),
        P(None, ("pass", "az"), "rg"),
        P(("pass", "az")),
        P(("pass", "az")),
        P(("pass", "az"), "rg"),
    )
    out_specs = (P(("pass", "az"), "rg"), P(("pass", "az"), "rg"))
    return jax.shard_map(
        on_device, mesh=mesh, in_specs=in_specs, out_specs=out_specs, check_vma=False
    )
```

```python
import functools
import math

import jax
import jax.numpy as jnp
import numpy as np
from jax import lax
from jax.experimental import pallas as pl
from jax.experimental.pallas import tpu as pltpu
from jax.sharding import PartitionSpec as P

LOOK_AZ = 4
LOOK_RG = 20
ITERS = 2


FULL_PRECISION = lax.Precision.HIGHEST
EPSILON = 1e-06


def from_behind(value, axis, steps):
    count = lax.axis_size(axis)
    first, last = (max(0, -steps), min(count, count - steps))
    return lax.ppermute(value, axis, [(source, source + steps) for source in range(first, last)])


def with_halo(shard, sides, width):
    for axis, dim in sides:
        peers, length = (lax.axis_size(axis), shard.shape[dim])
        up = [(i, (i + 1) % peers) for i in range(peers - 1)]
        down = [(j, i) for i, j in up]
        last = lax.slice_in_dim(shard, length - width, length, axis=dim)
        first = lax.slice_in_dim(shard, 0, width, axis=dim)
        before = lax.ppermute(last, axis, up)
        after = lax.ppermute(first, axis, down)
        shard = jnp.concatenate([before, shard, after], axis=dim)
    return shard


def dct_table(freq_index, place_index, length):
    product = (2 * place_index[None, :] + 1) * freq_index[:, None] % (4 * length)
    norm_factor = jnp.where(
        freq_index == 0, math.sqrt(1.0 / length), math.sqrt(2.0 / length)
    ).astype(jnp.float32)
    return norm_factor[:, None] * jnp.cos(product.astype(jnp.float32) * (math.pi / (2.0 * length)))


def eigenvalues(freq_index, length):
    return 4.0 * jnp.sin(freq_index.astype(jnp.float32) * (math.pi / (2.0 * length))) ** 2


def neighbours(padded):
    return (
        padded[..., :-2, 1:-1],
        padded[..., 2:, 1:-1],
        padded[..., 1:-1, :-2],
        padded[..., 1:-1, 2:],
    )


def contract(left, right, left_dim, right_dim):
    return lax.dot_general(
        left,
        right,
        (((left_dim,), (right_dim,)), ((), ())),
        precision=FULL_PRECISION,
        preferred_element_type=jnp.float32,
    )


CHUNK = 256


def look_kernel(lines, half, ref_ref, sec_ref, group_ref, line_ref, out_ref):
    step_rows = lines // LOOK_AZ
    width = half // LOOK_RG
    for side in range(out_ref.shape[2] // width):
        total = jnp.zeros((8 * lines, width), jnp.float32)
        for start in range(0, half, CHUNK):
            span = pl.ds(side * half + start, CHUNK)
            mr = ref_ref[0, :, span].astype(jnp.float32)
            mi = ref_ref[1, :, span].astype(jnp.float32)
            sr = sec_ref[0, :, span].astype(jnp.float32)
            si = sec_ref[1, :, span].astype(jnp.float32)
            planes = jnp.concatenate(
                [mr * sr + mi * si, mi * sr - mr * si, mr * mr + mi * mi, sr * sr + si * si], axis=0
            )
            high = planes.astype(jnp.bfloat16)
            low = (planes - high.astype(jnp.float32)).astype(jnp.bfloat16)
            total = total + jnp.dot(
                jnp.concatenate([high, low], axis=0),
                group_ref[pl.ds(start, CHUNK), :],
                preferred_element_type=jnp.float32,
            )
        joined = total[: 4 * lines] + total[4 * lines :]
        sums = jnp.dot(
            line_ref[...], joined, precision=FULL_PRECISION, preferred_element_type=jnp.float32
        )
        for plane in range(4):
            out_ref[plane, :, side * width : (side + 1) * width] = sums[
                plane * step_rows : (plane + 1) * step_rows
            ]


def form_looks(ref_lines, sec_lines, col_count):
    line_count, sample_count = ref_lines.shape[1:]
    lines = 32
    half = 128 * LOOK_RG
    group = (np.arange(half)[:, None] // LOOK_RG == np.arange(128)[None, :]).astype(jnp.bfloat16)
    line_of = (np.arange(4 * lines)[None, :] // LOOK_AZ == np.arange(lines)[:, None]).astype(
        np.float32
    )
    block = pl.BlockSpec((2, lines, sample_count), lambda i: (0, i, 0))
    return pl.pallas_call(
        functools.partial(look_kernel, lines, half),
        grid=(line_count // lines,),
        in_specs=[
            block,
            block,
            pl.BlockSpec(group.shape, lambda i: (0, 0)),
            pl.BlockSpec(line_of.shape, lambda i: (0, 0)),
        ],
        out_specs=pl.BlockSpec((4, lines // LOOK_AZ, col_count), lambda i: (0, i, 0)),
        out_shape=jax.ShapeDtypeStruct((4, line_count // LOOK_AZ, col_count), jnp.float32),
        name="form_looks",
    )(ref_lines, sec_lines, group, line_of)


class Exchange:
    def __init__(self, send_sems, recv_sems):
        self.send_sems, self.recv_sems = send_sems, recv_sems
        self.used = 0

    def copy(self, source, target, device):
        index = self.used
        self.used += 1
        return pltpu.make_async_remote_copy(
            src_ref=source,
            dst_ref=target,
            send_sem=self.send_sems.at[index],
            recv_sem=self.recv_sems.at[index],
            device_id=device,
            device_id_type=pl.DeviceIdType.MESH,
        )


def split(values):
    high = values.astype(jnp.bfloat16)
    rest = values - high.astype(jnp.float32)
    middle = rest.astype(jnp.bfloat16)
    return high, middle, (rest - middle.astype(jnp.float32)).astype(jnp.bfloat16)


def narrow_dot(left, right, dim):
    return lax.dot_general(
        left, right, (((1,), (dim,)), ((), ())), preferred_element_type=jnp.float32
    )


def pick_dot(choose, values):
    high, middle, low = [narrow_dot(choose, part, 0) for part in split(values)]
    return high + (middle + low)


def basis_dot(values, basis, dim):
    count = values.shape[0]
    high, middle, low = split(values)
    first = narrow_dot(jnp.concatenate([high, middle, low], axis=0), basis[0], dim)
    second = narrow_dot(jnp.concatenate([high, middle], axis=0), basis[1], dim)
    third = narrow_dot(high, basis[2], dim)
    small = first[2 * count :] + second[count:] + third
    return first[:count] + ((first[count : 2 * count] + second[:count]) + small)


LINES = 64


def form_block(index, width, ref_held, sec_held, group_ref, hold, looks):
    step_rows = LINES // LOOK_AZ
    lines = pl.ds(index * LINES, LINES)
    total = jnp.zeros((8 * step_rows, width), jnp.float32)
    for start in range(0, ref_held.shape[2], CHUNK):
        parts = []
        for begin in range(start, start + CHUNK, 128):
            span = pl.ds(begin, 128)
            slot = begin // 128
            mr = ref_held[0, lines, span].astype(jnp.float32)
            mi = ref_held[1, lines, span].astype(jnp.float32)
            sr = sec_held[0, lines, span].astype(jnp.float32)
            si = sec_held[1, lines, span].astype(jnp.float32)
            hold[slot, 0:LINES] = mr * sr + mi * si
            hold[slot, LINES : 2 * LINES] = mi * sr - mr * si
            hold[slot, 2 * LINES : 3 * LINES] = mr * mr + mi * mi
            hold[slot, 3 * LINES :] = sr * sr + si * si
            part = hold[slot, pl.ds(0, 4 * step_rows, stride=LOOK_AZ), :]
            for line in range(1, LOOK_AZ):
                part = part + hold[slot, pl.ds(line, 4 * step_rows, stride=LOOK_AZ), :]
            parts.append(part)
        sums = jnp.concatenate(parts, axis=1)
        high = sums.astype(jnp.bfloat16)
        low = (sums - high.astype(jnp.float32)).astype(jnp.bfloat16)
        total = total + jnp.dot(
            jnp.concatenate([high, low], axis=0),
            group_ref[pl.ds(start, CHUNK), :],
            preferred_element_type=jnp.float32,
        )
    joined = total[: 4 * step_rows] + total[4 * step_rows :]
    for plane in range(4):
        looks[plane, pl.ds(index * step_rows, step_rows), :] = joined[
            plane * step_rows : (plane + 1) * step_rows
        ]


def iota(shape, dim):
    return lax.broadcasted_iota(jnp.int32, shape, dim)


def unwrap_kernel(
    peers,
    capacity,
    damping,
    ref_ref,
    sec_ref,
    group_ref,
    target_ref,
    seam_row_ref,
    mask_ref,
    basis_ref,
    lam_row_ref,
    lam_col_ref,
    out_ref,
    ref_held,
    sec_held,
    hold,
    looks,
    load_sems,
    slot_send,
    slot_recv,
    place_send,
    place_recv,
    grid_own,
    grid_next,
    fields,
    spec_send,
    spec_recv,
    back_send,
    back_recv,
    dot_send,
    dot_recv,
    send_sems,
    recv_sems,
):
    me = lax.axis_index("az")
    core = lax.axis_index("rg")
    other = 1 - core
    last = peers - 1
    rows, cols = mask_ref.shape
    length = basis_ref.shape[1]
    slots = peers * capacity
    pencil = cols // peers
    exchange = Exchange(send_sems, recv_sems)
    sent = []

    def at(az, rg):
        return (lax.axis_index("pass"), az, rg)

    def ahead(offset):
        return lax.rem(me + offset, peers)

    def behind(offset):
        return lax.rem(me + peers - offset, peers)

    half = ref_held.shape[3]
    width = half // LOOK_RG
    blocks = rows * LOOK_AZ // LINES
    loads = {}
    for side in range(2):
        for index in range(blocks):
            for which, (source, target) in enumerate(((ref_ref, ref_held), (sec_ref, sec_held))):
                loads[side, index, which] = pltpu.make_async_copy(
                    source.at[:, pl.ds(index * LINES, LINES), pl.ds(side * half, half)],
                    target.at[side, :, pl.ds(index * LINES, LINES), :],
                    load_sems.at[side, index, which],
                )
                loads[side, index, which].start()

    def facing(offset):
        peer = me
        bit = 1
        while bit < peers:
            if offset & bit:
                peer = peer + bit - 2 * bit * (me // bit % 2)
            bit *= 2
        return peer

    barrier = pltpu.get_barrier_semaphore()
    for offset in range(peers):
        for side in (core, other):
            if offset or side is other:
                pl.semaphore_signal(
                    barrier,
                    inc=1,
                    device_id=at(ahead(offset), side),
                    device_id_type=pl.DeviceIdType.MESH,
                )

    def upright(line):
        diagonal = iota((rows, rows), 0) == iota((rows, rows), 1)
        return jnp.sum(jnp.where(diagonal, line, 0), axis=1, keepdims=True)

    target_row = target_ref[...]
    target_col = upright(target_row)
    owner_row = target_row // rows
    owner_col = target_col // rows
    same = owner_col == owner_row
    low_index = iota((rows, rows), 0)
    high_index = iota((rows, rows), 1)
    rank_row = jnp.sum(
        jnp.where(same & (low_index < high_index), 1, 0), axis=0, keepdims=True
    )
    rank_col = jnp.sum(
        jnp.where(same & (high_index < low_index), 1, 0), axis=1, keepdims=True
    )
    choose = jnp.where(
        iota((slots, rows), 0) == owner_row * capacity + rank_row, 1.0, 0.0
    ).astype(jnp.bfloat16)
    place = (target_col - owner_col * rows + 1).astype(jnp.float32)
    lane = iota((rows, slots), 1)
    here = lane == me * capacity + rank_col
    for dest in range(peers):
        line = jnp.sum(
            jnp.where(here & (owner_col == dest), place, 0.0), axis=0, keepdims=True
        )
        place_send[dest] = jnp.broadcast_to(line, (8, slots))
    pl.semaphore_wait(barrier, 2 * peers - 1)
    place_copies = []
    for offset in range(peers - 1, 0, -1):
        copy = exchange.copy(
            place_send.at[facing(offset)], place_recv.at[me], at(facing(offset), core)
        )
        copy.start()
        place_copies.append(copy)
    place_recv[me] = place_send[me]
    sent += place_copies
    slot_copies = []
    for side in range(2):
        for index in range(blocks):
            loads[side, index, 0].wait()
            loads[side, index, 1].wait()
            form_block(index, width, ref_held.at[side], sec_held.at[side], group_ref, hold, looks.at[side])
        joined = jnp.concatenate([looks[side, plane] for plane in range(4)], axis=1)
        chosen = pick_dot(choose, joined)
        for plane in range(4):
            slot_send[side, :, plane] = chosen[:, plane * width : (plane + 1) * width].reshape(
                peers, capacity, width
            )
        side_copies = []
        for offset in range(peers - 1, 0, -1):
            copy = exchange.copy(
                slot_send.at[side, facing(offset)],
                slot_recv.at[side, me],
                at(facing(offset), core),
            )
            copy.start()
            side_copies.append(copy)
        slot_recv[side, me] = slot_send[side, me]
        slot_copies.append(side_copies)
        sent += side_copies

    seam_pick = jnp.where(
        upright(seam_row_ref[...]) == iota((rows, rows), 1), 1.0, 0.0
    ).astype(jnp.bfloat16)
    for copy in place_copies:
        copy.wait_recv()
    places = place_recv[0]
    for source in range(1, peers):
        places = places + place_recv[source]
    scatter = jnp.where(
        places[0:1] == (iota((rows, slots), 0) + 1).astype(jnp.float32), 1.0, 0.0
    ).astype(jnp.bfloat16)
    seam_copies = []

    @pl.when(me == last)
    def _():
        grid_next[...] = jnp.zeros_like(grid_next)

    for side in range(2):
        for copy in slot_copies[side]:
            copy.wait_recv()
        gridded = pick_dot(
            scatter,
            jnp.concatenate(
                [slot_recv[side, :, plane].reshape(slots, width) for plane in range(4)], axis=1
            ),
        )
        grid_own[side] = gridded
        copy = exchange.copy(grid_own.at[side], grid_next.at[side], at(behind(1), core))

        @pl.when(me > 0)
        def _():
            copy.start()

        seam_copies.append(copy)

    own_lanes = pl.ds(pl.multiple_of(core * cols, cols), cols)
    fields[2, 8 : 8 + rows, own_lanes] = (1 + mask_ref[...]).astype(jnp.float32) * 0.25
    combined = []
    for side in range(2):

        @pl.when(me < last)
        def _():
            seam_copies[side].wait_recv()

        combined.append(grid_own[side] + pick_dot(seam_pick, grid_next[side]))
    combined = [
        jnp.concatenate([part[:, plane * width : (plane + 1) * width] for part in combined], axis=1)
        for plane in range(4)
    ]
    magnitude = jnp.sqrt(combined[2] * combined[3]) + EPSILON
    fields[0, 8 : 8 + rows, own_lanes] = combined[0] / magnitude
    fields[1, 8 : 8 + rows, own_lanes] = combined[1] / magnitude

    @pl.when(me == 0)
    def _():
        fields[:, 0:8, :] = jnp.zeros((3, 8, length), jnp.float32)

    @pl.when(me == last)
    def _():
        fields[:, 8 + rows :, :] = jnp.zeros((3, 8, length), jnp.float32)

    up_copies, down_copies = [], []
    for side in (core, other):
        up_copies.append(
            exchange.copy(
                fields.at[:, pl.ds(8, 8), own_lanes],
                fields.at[:, pl.ds(8 + rows, 8), own_lanes],
                at(behind(1), side),
            )
        )
        down_copies.append(
            exchange.copy(
                fields.at[:, pl.ds(rows, 8), own_lanes],
                fields.at[:, pl.ds(0, 8), own_lanes],
                at(ahead(1), side),
            )
        )

    @pl.when(me > 0)
    def _():
        for copy in up_copies:
            copy.start()

    @pl.when(me < last)
    def _():
        for copy in down_copies:
            copy.start()

    across = exchange.copy(
        fields.at[:, pl.ds(8, rows), own_lanes],
        fields.at[:, pl.ds(8, rows), own_lanes],
        at(me, other),
    )
    across.start()
    across.wait_recv()
    sent.append(across)

    @pl.when(me < last)
    def _():
        for copy in up_copies:
            copy.wait_recv()

    @pl.when(me > 0)
    def _():
        for copy in down_copies:
            copy.wait_recv()

    column = iota((rows, length), 1)

    def beside(values):
        middle = values[8 : 8 + rows]
        return (
            values[7 : 7 + rows],
            values[9 : 9 + rows],
            pltpu.roll(middle, 1, 1),
            pltpu.roll(middle, length - 1, 1),
        )

    weight = fields[2]
    inside = weight[8 : 8 + rows]
    edges = [inside * item for item in beside(weight)]
    edges[2] = jnp.where(column > 0, edges[2], 0.0)
    edges[3] = jnp.where(column < length - 1, edges[3], 0.0)
    real, imag = fields[0], fields[1]
    right_side = jnp.zeros((rows, length), jnp.float32)
    for edge, real_item, imag_item in zip(edges, beside(real), beside(imag)):
        right_side = right_side + edge * (
            imag[8 : 8 + rows] * real_item - real[8 : 8 + rows] * imag_item
        )

    def operator(values):
        middle = values[8 : 8 + rows]
        result = damping * middle
        for edge, item in zip(edges, beside(values)):
            result = result + edge * (middle - item)
        return result

    first_freq = pl.multiple_of(core * cols + me * pencil, pencil)
    divisor = lam_col_ref[pl.ds(first_freq, pencil), :] + lam_row_ref[...] + damping

    def gather_dots(turn, values):
        row = iota((8, 128), 0)
        tile = jnp.zeros((8, 128), jnp.float32)
        for index, value in enumerate(values):
            tile = jnp.where(row == index, jnp.sum(value, keepdims=True), tile)
        dot_send[turn] = tile
        dot_recv[turn, me] = tile
        copies = []
        for offset in range(peers - 1, 0, -1):
            copy = exchange.copy(
                dot_send.at[turn], dot_recv.at[turn, me], at(facing(offset), core)
            )
            copy.start()
            copies.append(copy)
        sent.extend(copies)

        def finish():
            for copy in copies:
                copy.wait_recv()
            total = dot_recv[turn, 0]
            for source in range(1, peers):
                total = total + dot_recv[turn, source]
            return [total[index : index + 1, 0:1] for index in range(len(values))]

        return finish

    basis = [basis_ref[part] for part in range(3)]

    def precondition(turn, values, meanwhile):
        half_basis = [basis_ref[part, own_lanes, :] for part in range(3)]
        spectrum = basis_dot(values, half_basis, 1).T
        half = pencil // 2
        for dest in range(peers):
            base = dest * pencil
            spec_send[turn, dest] = jnp.concatenate(
                [spectrum[base : base + half], spectrum[base + half : base + pencil]], axis=1
            )
        copies = []
        for offset in range(peers - 1, 0, -1):
            copy = exchange.copy(
                spec_send.at[turn, facing(offset)],
                spec_recv.at[turn, me],
                at(facing(offset), core),
            )
            copy.start()
            copies.append(copy)
        spec_recv[turn, me] = spec_send[turn, me]
        extra = meanwhile()
        for copy in copies:
            copy.wait_recv()
        sent.extend(copies)
        blocks = [spec_recv[turn, source] for source in range(peers)]
        columns = jnp.concatenate(
            [
                jnp.concatenate([block[:, :rows] for block in blocks], axis=1),
                jnp.concatenate([block[:, rows:] for block in blocks], axis=1),
            ],
            axis=0,
        )
        filtered = basis_dot(columns, basis, 1) / divisor
        restored = basis_dot(filtered, basis, 0)
        margin = jnp.zeros((pencil, rows // 2), jnp.float32)
        padded = jnp.concatenate([margin, restored, margin], axis=1)
        for dest in range(peers):
            back_send[turn, dest] = padded[:, dest * rows : (dest + 2) * rows]
        copies = []
        for offset in range(peers - 1, 0, -1):
            copy = exchange.copy(
                back_send.at[turn, facing(offset)],
                back_recv.at[turn, core, me],
                at(facing(offset), core),
            )
            copy.start()
            copies.append(copy)
        back_recv[turn, core, me] = back_send[turn, me]
        relays = [
            exchange.copy(
                back_send.at[turn, me], back_recv.at[turn, core, me], at(me, other)
            )
        ]
        relays[0].start()
        for offset in range(1, peers):
            copies[peers - 1 - offset].wait_recv()
            held = back_recv.at[turn, core, facing(offset)]
            relay = exchange.copy(held, held, at(me, other))
            relay.start()
            relays.append(relay)
        for relay in relays:
            relay.wait_recv()
        sent.extend(copies + relays)
        window = back_recv[turn].reshape(length, 2 * rows).T
        start = rows // 2 - 8
        return basis_dot(window[start : start + rows + 16], basis, 0), extra

    z0, _ = precondition(0, right_side, lambda: None)
    z0_mid = z0[8 : 8 + rows]
    w0 = operator(z0)
    y0, finish = precondition(
        1, w0, lambda: gather_dots(0, [right_side * z0_mid, z0_mid * w0])
    )
    rho0, energy0 = finish()
    alpha0 = rho0 / energy0
    r1 = right_side - alpha0 * w0
    z1 = z0 - alpha0 * y0
    z1_mid = z1[8 : 8 + rows]
    q1 = operator(z1)
    rho1, energy1, cross = gather_dots(1, [r1 * z1_mid, z1_mid * q1, z0_mid * q1])()
    beta = rho1 / rho0
    alpha1 = rho1 / (energy1 + 2.0 * beta * cross + beta * beta * energy0)
    answer = alpha0 * z0_mid + alpha1 * (z1_mid + beta * z0_mid)
    left = r1 - alpha1 * (q1 + beta * w0)
    out_ref[0] = jnp.where(core == 0, answer[:, :cols], answer[:, cols:])
    out_ref[1] = jnp.where(core == 0, left[:, :cols], left[:, cols:])

    for copy in sent:
        copy.wait_send()

    @pl.when(me > 0)
    def _():
        for copy in seam_copies + up_copies:
            copy.wait_send()

    @pl.when(me < last)
    def _():
        for copy in down_copies:
            copy.wait_send()


def fits_kernel(peers, cores, rows, cols):
    length = rows * peers
    capacity = max(2, 2 * rows // peers)
    return (
        cores == 2
        and rows == 64
        and length == cols * cores
        and length <= 1024
        and peers * capacity == 128
        and cols % (16 * peers) == 0
        and cols == 256
        and peers & (peers - 1) == 0
    )


def unwrap_in_kernel(reference_slc, secondary_slc, line_target, seam_partner, mask_level, peers):
    rows, cols = mask_level.shape
    length = rows * peers
    capacity = max(2, 2 * rows // peers)
    damping = 0.25 / (rows * rows)
    freq = np.arange(length)
    angle = (2 * freq[None, :] + 1) * freq[:, None] % (4 * length)
    basis = np.sqrt(np.where(freq == 0, 1.0, 2.0) / length)[:, None] * np.cos(
        angle * (math.pi / (2.0 * length))
    )
    lam = 4.0 * np.sin(freq * (math.pi / (2.0 * length))) ** 2
    pencil = cols // peers
    half = reference_slc.shape[2] // 2
    width = half // LOOK_RG
    group = (np.arange(half)[:, None] // LOOK_RG == np.arange(width)[None, :]).astype(jnp.bfloat16)
    parts, rest = [], basis
    for _ in range(3):
        parts.append(rest.astype(jnp.bfloat16))
        rest = rest - parts[-1].astype(np.float64)
    hbm = pl.BlockSpec(memory_space=pl.ANY)
    copies = 2 * (peers - 1) + (peers - 1) + 2 + 5 + 2 * (3 * (peers - 1) + 1) + 2 * (peers - 1)
    vmem = pl.BlockSpec(memory_space=pltpu.VMEM)

    def scratch(*dims):
        return pltpu.VMEM(dims, jnp.float32)

    both = pl.pallas_call(
        functools.partial(unwrap_kernel, peers, capacity, damping),
        out_shape=jax.ShapeDtypeStruct((2, rows, cols), jnp.float32),
        in_specs=[hbm] * 2 + [vmem] * 7,
        out_specs=vmem,
        scratch_shapes=[
            pltpu.VMEM((2, 2, rows * LOOK_AZ, half), jnp.bfloat16),
            pltpu.VMEM((2, 2, rows * LOOK_AZ, half), jnp.bfloat16),
            scratch(half // 128, 4 * LINES, 128),
            scratch(2, 4, rows, width),
            pltpu.SemaphoreType.DMA((2, rows * LOOK_AZ // LINES, 2)),
            scratch(2, peers, 4, capacity, width),
            scratch(2, peers, 4, capacity, width),
            scratch(peers, 8, 128),
            scratch(peers, 8, 128),
            scratch(2, rows, 4 * width),
            scratch(2, rows, 4 * width),
            scratch(3, rows + 16, length),
            scratch(2, peers, pencil // 2, 2 * rows),
            scratch(2, peers, pencil // 2, 2 * rows),
            scratch(2, peers, pencil, 2 * rows),
            scratch(2, 2, peers, pencil, 2 * rows),
            scratch(2, 8, 128),
            scratch(2, peers, 8, 128),
            pltpu.SemaphoreType.DMA((copies,)),
            pltpu.SemaphoreType.DMA((copies,)),
        ],
        compiler_params=pltpu.CompilerParams(collective_id=0, has_side_effects=True),
        name="unwrap",
    )(
        reference_slc,
        secondary_slc,
        group,
        line_target.reshape(1, rows),
        seam_partner.reshape(1, rows),
        mask_level,
        np.stack(parts),
        lam.astype(np.float32)[None, :],
        lam.astype(np.float32)[:, None],
    )
    shape = jax.ShapeDtypeStruct((rows, cols), jnp.float32)
    return pl.pallas_call(
        part_kernel,
        out_shape=(shape, shape),
        in_specs=[vmem],
        out_specs=(vmem, vmem),
        name="part",
    )(both)


def part_kernel(both_ref, first_ref, second_ref):
    first_ref[...] = both_ref[0]
    second_ref[...] = both_ref[1]


def single_product(left, right):
    return lax.psum(jnp.sum(left * right), ("az", "rg"))


def on_device(reference_slc, secondary_slc, line_target, seam_partner, mask_level):
    dev_count = lax.axis_size("az")
    rg_count = lax.axis_size("rg")
    az_place = lax.axis_index("az")
    rg_place = lax.axis_index("rg")
    row_count = line_target.shape[0]
    col_count = mask_level.shape[1]
    if fits_kernel(dev_count, rg_count, row_count, col_count):
        return unwrap_in_kernel(
            reference_slc, secondary_slc, line_target, seam_partner, mask_level, dev_count
        )
    local_sums = form_looks(reference_slc, secondary_slc, col_count)
    capacity = max(2, 2 * row_count // dev_count)
    owners = line_target // row_count
    local_index = jnp.arange(row_count, dtype=jnp.int32)
    earlier = (owners[:, None] == owners[None, :]) & (local_index[None, :] < local_index[:, None])
    slot_rank = jnp.sum(earlier.astype(jnp.int32), axis=1)
    slot_index = owners * capacity + slot_rank
    buffer_length = dev_count * capacity
    source_row = jnp.full((buffer_length,), row_count, jnp.int32).at[slot_index].set(local_index)
    positions = (
        jnp.full((1, buffer_length), row_count, jnp.int32)
        .at[0, slot_index]
        .set(line_target % row_count)
    )
    sent_sums = jnp.take(local_sums, source_row, axis=1, mode="fill", fill_value=0.0)
    got_sums, got_positions = (
        lax.all_to_all(sent_sums, "az", split_axis=1, concat_axis=1, tiled=True),
        lax.all_to_all(positions, "az", split_axis=1, concat_axis=1, tiled=True),
    )
    gridded = jnp.zeros_like(local_sums).at[:, got_positions[0]].set(got_sums, mode="drop")
    next_block = from_behind(gridded, "az", -1)
    has_partner = seam_partner >= 0
    picked = jnp.take(next_block, jnp.maximum(seam_partner, 0), axis=1)
    combined = gridded + jnp.where(has_partner[None, :, None], picked, 0.0)
    magnitude = jnp.sqrt(combined[2] * combined[3]) + EPSILON
    weight = (1 + mask_level).astype(jnp.float32) * 0.25
    fields = jnp.stack([combined[0] / magnitude, combined[1] / magnitude, weight])
    padded = with_halo(fields, (("az", 1), ("rg", 2)), 1)
    beside_all = neighbours(padded)
    edge_weights = [weight * item[2] for item in beside_all]
    right_side = jnp.zeros((row_count, col_count), jnp.float32)
    for edge, item in zip(edge_weights, beside_all):
        right_side = right_side + edge * (fields[1] * item[0] - fields[0] * item[1])
    damping = 0.25 / (row_count * row_count)
    grid_rows = row_count * dev_count
    grid_cols = col_count * rg_count
    my_cols = rg_place * col_count + jnp.arange(col_count, dtype=jnp.int32)
    column_width = col_count // dev_count
    all_rows = jnp.arange(grid_rows, dtype=jnp.int32)
    full_basis = dct_table(all_rows, all_rows, grid_rows)
    pencil_cols = (
        rg_place * col_count + az_place * column_width + jnp.arange(column_width, dtype=jnp.int32)
    )
    pencil_divisor = (
        eigenvalues(pencil_cols, grid_cols)[:, None]
        + eigenvalues(all_rows, grid_rows)[None, :]
        + damping
    )

    def precondition(values):
        basis_block = dct_table(
            jnp.arange(col_count * lax.axis_size("rg"), dtype=jnp.int32), my_cols, grid_cols
        )
        range_spectrum = lax.psum_scatter(
            contract(basis_block, values, 1, 1), "rg", scatter_dimension=0, tiled=True
        )
        pencil = lax.all_to_all(range_spectrum, "az", split_axis=0, concat_axis=1, tiled=True)
        filtered = contract(pencil, full_basis, 1, 1) / pencil_divisor
        restored = contract(filtered, full_basis, 1, 0)
        back_columns = lax.all_to_all(restored, "az", split_axis=1, concat_axis=0, tiled=True)
        basis_block = dct_table(
            my_cols, jnp.arange(col_count * lax.axis_size("rg"), dtype=jnp.int32), grid_cols
        )
        return lax.psum_scatter(
            contract(basis_block, back_columns, 0, 0), "rg", scatter_dimension=0, tiled=True
        ).T

    solution = jnp.zeros((row_count, col_count), jnp.float32)
    residual = right_side
    precond = precondition(residual)
    direction = precond
    inner_now = single_product(residual, precond)
    for turn_index in range(ITERS):
        rim = with_halo(direction, (("az", 0), ("rg", 1)), 1)
        result_sum = damping * direction
        for apply_edge, apply_item in zip(edge_weights, neighbours(rim)):
            result_sum = result_sum + apply_edge * (direction - apply_item)
        step_size = inner_now / lax.psum(jnp.sum(direction * result_sum), ("az", "rg"))
        solution = solution + step_size * direction
        residual = residual - step_size * result_sum
        if turn_index + 1 < ITERS:
            precond = precondition(residual)
            inner_next = single_product(residual, precond)
            direction = precond + inner_next / inner_now * direction
            inner_now = inner_next
    return (solution, residual)


def solution(mesh):
    in_specs = (
        P(None, ("pass", "az"), "rg"),
        P(None, ("pass", "az"), "rg"),
        P(("pass", "az")),
        P(("pass", "az")),
        P(("pass", "az"), "rg"),
    )
    out_specs = (P(("pass", "az"), "rg"), P(("pass", "az"), "rg"))
    return jax.shard_map(
        on_device, mesh=mesh, in_specs=in_specs, out_specs=out_specs, check_vma=False
    )
```
